128 devices in a mesh: outer: 16 (over x, y), inner: 8 (over z, core).
Axes of the slice: x: 4, y: 4, z: 4, core: 2. Of those that a mesh axis runs over, the one named last changes fastest.
Arguments:
- queries: bfloat16 [24, 131072, 128], P(None, ('outer', 'inner')), may hold values from -6 to 6
- keys: bfloat16 [24, 131072, 128], P(None, ('outer', 'inner')), may hold values from -6 to 6
- values: bfloat16 [24, 131072, 128], P(None, ('outer', 'inner')), may hold values from -6 to 6
- starts: int32 [128], P(('outer', 'inner')), may hold values from 0 to 1024, as said below
- lengths: int32 [128], P(('outer', 'inner')), may hold values from 0 to 65535, as said below
Outputs:
- attended: bfloat16 [24, 131072, 128], P(None, ('outer', 'inner'))
The draws below stay inside these ranges and needn't reach their ends.
Inputs may be any that keep to these rules, and one draw needn't show every extreme that they name: `starts`: the value 1024 means that no prompt begins in the block; block 0 has a prompt beginning at offset 0; every prompt but the last in the sequence has between 8192 and 65536 positions, so at most one prompt begins in a block. `lengths`: consistent with starts: the number of positions from the beginning of the prompt holding the block's first position up to that position; no prompt has more than 65536 positions.
All inputs are finite; a program needn't handle non-finite values.
Results may differ from the reference program's by a relative error of at most 0.005.
Values sent between devices are 32-bit elements; how exact they have to be, the bound alone decides.
No kernel may reach another device: no remote copies, remote signals or barrier semaphores. Data moves between devices by JAX's collectives and lax.ppermute only.
A program may use at most 128 MiB of HBM per device.

```python
import math
import jax
import jax.numpy as jnp
from jax import lax

H = 24
DH = 128
TOK_DEV = 1024
TOKENS = 131072


def prompt_plan(key):
    blocks = TOKENS // TOK_DEV
    sizes_drawn = jax.random.randint(jax.random.fold_in(key, 7), (17,), TOKENS // 16, TOKENS // 2 + 1, dtype=jnp.int32)
    first_blocks = jax.random.randint(jax.random.fold_in(key, 11), (1,), TOKENS // 16 // TOK_DEV, TOKENS // 2 // TOK_DEV, dtype=jnp.int32)
    first_size = first_blocks * TOK_DEV + 1
    second_size = jnp.full((1,), TOKENS // 2, dtype=jnp.int32)
    sizes_drawn = jnp.concatenate([first_size, second_size, sizes_drawn[2:]]).astype(jnp.int32)
    begins = jnp.cumsum(sizes_drawn) - sizes_drawn
    block_edges = jnp.arange(blocks, dtype=jnp.int32) * TOK_DEV
    inside = (begins[None, :] >= block_edges[:, None]) & (begins[None, :] < block_edges[:, None] + TOK_DEV)
    offset_sum = jnp.sum(jnp.where(inside, begins[None, :] - block_edges[:, None], 0), axis=1)
    new_starts = jnp.where(jnp.any(inside, axis=1), offset_sum, TOK_DEV).astype(jnp.int32)
    latest = jnp.max(jnp.where(begins[None, :] <= block_edges[:, None], begins[None, :], 0), axis=1)
    before = (block_edges - latest).astype(jnp.int32)
    return (new_starts, before)


def draw_starts(key, part):
    return prompt_plan(key)[0]


def draw_lengths(key, part):
    return prompt_plan(key)[1]


def levels(own_key, extent, cuts, smallest, high):
    def one(dim, shards_of):
        heights = jax.random.uniform(jax.random.fold_in(jax.random.fold_in(own_key, 6), dim), (shards_of,), jnp.float32, smallest / len(cuts), high / len(cuts))
        return jnp.repeat(jnp.exp(heights), extent[dim] // shards_of).reshape((-1,) + (1,) * (len(extent) - dim - 1))

    loudness = one(*cuts[0])
    for cut in cuts[1:]:
        loudness = loudness * one(*cut)
    return loudness


def centred(stream_key, extent, width, reach, shards=(), held_as=jnp.bfloat16):
    array = jax.random.normal(stream_key, extent, jnp.float32) * width
    if len(shards) > 0:
        array = levels(stream_key, extent, shards, -0.22, 0.18) * array
    return jnp.clip(array, min=-reach, max=reach).astype(held_as)


def setup_inputs(seed: int = 0) -> dict:
    arg_keys = jax.random.split(jax.random.key(seed), 6)
    queries = centred(arg_keys[0], (H, TOKENS, DH), 1.0, 6.0, ((1, 128),))
    keys = centred(arg_keys[1], (H, TOKENS, DH), 1.0, 6.0, ((1, 128),))
    values = centred(arg_keys[2], (H, TOKENS, DH), 1.0, 6.0, ((1, 128),))
    starts = draw_starts(jax.random.fold_in(arg_keys[5], 71), 0)
    lengths = draw_lengths(jax.random.fold_in(arg_keys[5], 71), 0)
    return {"queries": queries, "keys": keys, "values": values, "starts": starts, "lengths": lengths}


def combine(earlier, later):
    return (jnp.where(later[1] > 0.5, later[0], earlier[0] + later[0]), jnp.maximum(earlier[1], later[1]))

def reference(queries, keys, values, starts, lengths):
    score_scale = 1.0 / math.sqrt(DH)
    blocks = TOKENS // TOK_DEV
    query_blocks = queries.reshape(H, blocks, TOK_DEV, DH).transpose(1, 0, 2, 3)
    key_blocks = keys.reshape(H, blocks, TOK_DEV, DH).transpose(1, 0, 2, 3)
    value_blocks = values.reshape(H, blocks, TOK_DEV, DH).transpose(1, 0, 2, 3)
    offsets = jnp.arange(TOK_DEV, dtype=jnp.int32)

    def block_state(pieces):
        key_rows, value_rows, new_start = pieces
        begin = jnp.where(new_start < TOK_DEV, new_start, 0)
        kept_rows = (offsets >= begin).astype(jnp.float32)
        return jnp.einsum('hsd,hse->hde', key_rows.astype(jnp.float32) * kept_rows[None, :, None], value_rows.astype(jnp.float32))
    states = lax.map(block_state, (key_blocks, value_blocks, starts))
    resets = (starts < TOK_DEV).astype(jnp.float32)

    def advance(carried_sum, pieces):
        return (combine(carried_sum, pieces), carried_sum)
    initial = (jnp.zeros((H, DH, DH), jnp.float32), jnp.zeros((), jnp.float32))
    unused, carried = lax.scan(advance, initial, (states, resets))
    carried_states = carried[0]

    def block_output(pieces):
        query_rows, key_rows, value_rows, new_start, length, carried_sum = pieces
        earlier = offsets < new_start
        allowed = (earlier[:, None] == earlier[None, :]) & (offsets[None, :] <= offsets[:, None])
        scores = jnp.einsum('hcd,hsd->hcs', query_rows.astype(jnp.float32), key_rows.astype(jnp.float32)) * score_scale
        scores = lax.optimization_barrier(jnp.where(allowed[None], scores, 0.0).astype(jnp.bfloat16))
        inside = jnp.einsum('hcs,hsd->hcd', scores.astype(jnp.float32), value_rows.astype(jnp.float32))
        rounded = lax.optimization_barrier(carried_sum.astype(jnp.bfloat16))
        across = jnp.einsum('hcd,hde->hce', query_rows.astype(jnp.float32), rounded.astype(jnp.float32)) * score_scale
        across = across * earlier[None, :, None]
        counts = jnp.where(earlier, length + offsets + 1, offsets - new_start + 1).astype(jnp.float32)
        return ((inside + across) / jnp.sqrt(counts)[None, :, None]).astype(jnp.bfloat16)
    outputs = lax.map(block_output, (query_blocks, key_blocks, value_blocks, starts, lengths, carried_states))
    return outputs.transpose(1, 0, 2, 3).reshape(H, TOKENS, DH)
```

```python
import functools
import math

import jax
import jax.numpy as jnp
import numpy as np
from jax import lax
from jax.experimental import pallas as pl
from jax.experimental.pallas import tpu as pltpu
from jax.sharding import Mesh
from jax.sharding import PartitionSpec as P

CHUNK = 256
MIB = 1 << 20


def rows_of(first, shape):
    return first + lax.broadcasted_iota(jnp.int32, shape, 0)


def state_kernel(flagged, heads, scalars, k_ref, v_ref, s_ref, mask_ref):
    step = pl.program_id(0)
    length, width = k_ref.shape[1], k_ref.shape[2]
    start = scalars[0]

    @pl.when(step == 0)
    def _():
        begin = jnp.where(start < length, start, 0)
        kept = rows_of(0, (length, width)) >= begin
        mask_ref[...] = jnp.where(kept, 1.0, 0.0).astype(mask_ref.dtype)
        if flagged:
            flag = jnp.where(start < length, 1.0, 0.0)
            s_ref[-8:, :] = jnp.full((8, width), flag, jnp.float32)

    for h in range(heads):
        state = lax.dot_general(
            k_ref[h] * mask_ref[...],
            v_ref[h],
            (((0,), (0,)), ((), ())),
            preferred_element_type=jnp.float32,
        )
        first = pl.multiple_of((step * heads + h) * width, width)
        s_ref[pl.ds(first, width), :] = state


def block_states(scalars, keys, values, slot, flagged, heads=3):
    count, length, width = keys.shape
    steps = count // 2 // heads
    spec = pl.BlockSpec((heads, length, width), lambda i, s: (s[slot] * steps + i, 0, 0))
    rows = count // 2 * width + (8 if flagged else 0)
    return pl.pallas_call(
        functools.partial(state_kernel, flagged, heads),
        out_shape=jax.ShapeDtypeStruct((rows, width), jnp.float32),
        grid_spec=pltpu.PrefetchScalarGridSpec(
            num_scalar_prefetch=1,
            grid=(steps,),
            in_specs=[spec, spec],
            out_specs=pl.BlockSpec((rows, width), lambda i, s: (0, 0)),
            scratch_shapes=[pltpu.VMEM((length, width), jnp.bfloat16)],
        ),
        compiler_params=pltpu.CompilerParams(vmem_limit_bytes=16 * MIB),
        cost_estimate=pl.CostEstimate(
            flops=count * length * width * width,
            bytes_accessed=count * length * width * 2,
            transcendentals=0,
        ),
        name="states",
    )(scalars, keys, values)


def chip_kernel(scalars, own_ref, got_ref, out_ref):
    first = scalars[2] == 0
    own_reset = jnp.where(scalars[0] < scalars[3], 1.0, 0.0)
    got_reset = got_ref[-8:, :]
    own_part = jnp.where(first, 1.0 - got_reset, 1.0)
    got_part = jnp.where(first, 1.0, 1.0 - own_reset)
    slices, rows, width = out_ref.shape
    data = rows - 8
    own = own_ref[...].reshape(slices * data // 8, 8, width)
    got = got_ref[: slices * data, :].reshape(slices * data // 8, 8, width)
    total = own * own_part[None] + got * got_part
    out_ref[:, :data, :] = total.reshape(slices, data, width)
    mark = jnp.maximum(got_reset, own_reset)
    out_ref[:, data:, :] = jnp.broadcast_to(mark[None], (slices, 8, width))


def chip_states(scalars, own, got, slices):
    rows, width = own.shape
    return pl.pallas_call(
        chip_kernel,
        out_shape=jax.ShapeDtypeStruct((slices, rows // slices + 8, width), jnp.float32),
        in_specs=[
            pl.BlockSpec(memory_space=pltpu.SMEM),
            pl.BlockSpec(memory_space=pltpu.VMEM),
            pl.BlockSpec(memory_space=pltpu.VMEM),
        ],
        out_specs=pl.BlockSpec(memory_space=pltpu.VMEM),
        compiler_params=pltpu.CompilerParams(vmem_limit_bytes=16 * MIB),
        name="chip_states",
    )(scalars, own, got)


def scan_kernel(part_ref, out_ref):
    slices, data, width = out_ref.shape

    def turn(c, before):
        out_ref[c] = before
        part = part_ref[c]
        reset = part[data:, :]
        kept = before.reshape(data // 8, 8, width) * (1.0 - reset)[None]
        return kept.reshape(data, width) + part[:data, :]

    lax.fori_loop(0, slices, turn, jnp.zeros((data, width), jnp.float32), unroll=8)


def scan_chips(parts):
    slices, rows, width = parts.shape
    return pl.pallas_call(
        scan_kernel,
        out_shape=jax.ShapeDtypeStruct((slices, rows - 8, width), jnp.float32),
        in_specs=[pl.BlockSpec(memory_space=pltpu.VMEM)],
        out_specs=pl.BlockSpec(memory_space=pltpu.VMEM),
        compiler_params=pltpu.CompilerParams(vmem_limit_bytes=16 * MIB),
        name="scan_chips",
    )(parts)


def core_kernel(scalars, before_ref, own_ref, got_ref, mine_ref, send_ref):
    first = scalars[2] == 0
    rows, width = own_ref.shape
    shape = (rows // 8, 8, width)
    own_reset = jnp.where(scalars[0] < scalars[3], 1.0, 0.0)
    reset = jnp.where(first, own_reset, got_ref[rows:, :])
    before = before_ref[...].reshape(shape)
    state = jnp.where(first, own_ref[...], got_ref[:rows, :]).reshape(shape)
    after = before * (1.0 - reset)[None] + state
    mine_ref[...] = jnp.where(first, before, after).reshape(rows, width)
    send_ref[...] = jnp.where(first, after, before).reshape(rows, width)


def core_carried(scalars, before, own, got):
    rows, width = own.shape
    out = jax.ShapeDtypeStruct((rows, width), jnp.float32)
    vmem = pl.BlockSpec(memory_space=pltpu.VMEM)
    return pl.pallas_call(
        core_kernel,
        out_shape=(out, out),
        in_specs=[pl.BlockSpec(memory_space=pltpu.SMEM), vmem, vmem, vmem],
        out_specs=(vmem, vmem),
        compiler_params=pltpu.CompilerParams(vmem_limit_bytes=16 * MIB),
        name="core_carried",
    )(scalars, before, own, got)


def inverse_roots(start, length, rows, width):
    offsets = rows_of(0, (rows, width))
    counts = jnp.where(offsets < start, length + offsets + 1, offsets - start + 1)
    return 1.0 / jnp.sqrt(counts.astype(jnp.float32))


def inside_kernel(
    heads, scale, scalars, q_ref, k_ref, v_ref, o_ref, pair_ref, query_ref, key_ref, root_ref
):
    start, length = scalars[0], scalars[1]
    rows, width = q_ref.shape[1], q_ref.shape[2]
    chunks = rows // CHUNK

    @pl.when(pl.program_id(0) == 0)
    def _():
        root_ref[...] = inverse_roots(start, length, rows, width)
        for i in range(chunks):
            low = i * CHUNK
            inner = (start >= low) & (start < low + CHUNK)
            t = rows_of(low, (CHUNK, CHUNK))
            s = low + lax.broadcasted_iota(jnp.int32, (CHUNK, CHUNK), 1)
            allowed = (s <= t) & ((t < start) == (s < start))
            pair_ref[i] = jnp.where(allowed, scale, 0.0)
            t = rows_of(low, (CHUNK, width))
            cut = jnp.where(inner, start, low + CHUNK)
            query_ref[i] = jnp.where(t < cut, 1.0, 0.0)
            begin = jnp.where(inner, start, low)
            key_ref[i] = jnp.where(t >= begin, 1.0, 0.0).astype(key_ref.dtype)

    for h in range(heads):
        state = None
        for i in range(chunks):
            low = i * CHUNK
            here = slice(low, low + CHUNK)
            q, k, v = q_ref[h, here, :], k_ref[h, here, :], v_ref[h, here, :]
            scores = lax.dot_general(
                q, k, (((1,), (1,)), ((), ())), preferred_element_type=jnp.float32
            )
            scores = (scores * pair_ref[i]).astype(jnp.bfloat16)
            total = jnp.dot(scores, v, preferred_element_type=jnp.float32)
            if i > 0:
                past = (state * scale).astype(jnp.bfloat16)
                total += jnp.dot(q, past, preferred_element_type=jnp.float32) * query_ref[i]
            o_ref[h, here, :] = (total * root_ref[here, :]).astype(o_ref.dtype)
            if i < chunks - 1:
                new = lax.dot_general(
                    k * key_ref[i],
                    v,
                    (((0,), (0,)), ((), ())),
                    preferred_element_type=jnp.float32,
                )
                inner = (start >= low) & (start < low + CHUNK)
                state = new if i == 0 else new + state * jnp.where(inner, 0.0, 1.0)


def inside(scalars, queries, keys, values, scale, heads=2):
    count, rows, width = queries.shape
    chunks = rows // CHUNK
    spec = pl.BlockSpec((heads, rows, width), lambda i, s: (i, 0, 0))
    return pl.pallas_call(
        functools.partial(inside_kernel, heads, scale),
        out_shape=jax.ShapeDtypeStruct(queries.shape, jnp.float32),
        grid_spec=pltpu.PrefetchScalarGridSpec(
            num_scalar_prefetch=1,
            grid=(count // heads,),
            in_specs=[spec, spec, spec],
            out_specs=spec,
            scratch_shapes=[
                pltpu.VMEM((chunks, CHUNK, CHUNK), jnp.float32),
                pltpu.VMEM((chunks, CHUNK, width), jnp.float32),
                pltpu.VMEM((chunks, CHUNK, width), jnp.bfloat16),
                pltpu.VMEM((rows, width), jnp.float32),
            ],
        ),
        compiler_params=pltpu.CompilerParams(vmem_limit_bytes=24 * MIB),
        cost_estimate=pl.CostEstimate(
            flops=count * rows * width * (4 * CHUNK + 4 * width),
            bytes_accessed=count * rows * width * 10,
            transcendentals=0,
        ),
        name="inside",
    )(scalars, queries, keys, values)


def across_kernel(heads, scale, scalars, q_ref, o_ref, c_ref, *rest):
    out_ref, weight_ref = rest[-2:]
    start, length = scalars[0], scalars[1]
    rows, width = q_ref.shape[1], q_ref.shape[2]

    @pl.when(pl.program_id(0) == 0)
    def _():
        weight = inverse_roots(start, length, rows, width) * scale
        weight_ref[...] = jnp.where(rows_of(0, (rows, width)) < start, weight, 0.0)

    for h in range(heads):
        carried = c_ref[h * width : (h + 1) * width, :].astype(jnp.bfloat16)
        across = jnp.dot(q_ref[h], carried, preferred_element_type=jnp.float32)
        out_ref[h] = (o_ref[h] + across * weight_ref[...]).astype(out_ref.dtype)


def add_across(scalars, queries, partial, carried, slot, scale, before=None, heads=3):
    count, rows, width = queries.shape
    steps = count // 2 // heads
    spec = pl.BlockSpec((heads, rows, width), lambda i, s: (s[slot] * steps + i, 0, 0))
    in_specs = [spec, spec, pl.BlockSpec((heads * width, width), lambda i, s: (i, 0))]
    operands = [scalars, queries, partial, carried]
    aliases = {}
    if before is not None:
        in_specs.append(pl.BlockSpec(memory_space=pl.ANY))
        operands.append(before)
        aliases = {4: 0}
    return pl.pallas_call(
        functools.partial(across_kernel, heads, scale),
        out_shape=jax.ShapeDtypeStruct(queries.shape, jnp.bfloat16),
        grid_spec=pltpu.PrefetchScalarGridSpec(
            num_scalar_prefetch=1,
            grid=(steps,),
            in_specs=in_specs,
            out_specs=spec,
            scratch_shapes=[pltpu.VMEM((rows, width), jnp.float32)],
        ),
        input_output_aliases=aliases,
        compiler_params=pltpu.CompilerParams(vmem_limit_bytes=24 * MIB),
        cost_estimate=pl.CostEstimate(
            flops=count * rows * width * width,
            bytes_accessed=count * rows * width * 4,
            transcendentals=0,
        ),
        name="across",
    )(*operands)


def shards(queries, keys, values, starts, lengths):
    count, rows, width = queries.shape
    scale = 1.0 / math.sqrt(width)
    chips = lax.axis_size("outer") * lax.axis_size("z")
    core = lax.axis_index("core").astype(jnp.int32)
    scalars = jnp.stack([starts[0], lengths[0], core, jnp.int32(rows), 1 - core])
    swap = [(0, 1), (1, 0)]

    theirs = block_states(scalars, keys, values, 4, True)
    got = lax.ppermute(theirs, "core", swap)
    own = block_states(scalars, keys, values, 2, False)
    parts = chip_states(scalars, own, got, chips)
    parts = lax.all_to_all(parts, ("outer", "z"), 0, 0, tiled=True)
    partial = inside(scalars, queries, keys, values, scale)
    befores = scan_chips(parts)
    before = lax.all_to_all(befores, ("outer", "z"), 0, 0, tiled=True)
    before = before.reshape(own.shape)
    mine, send = core_carried(scalars, before, own, got)
    rest = lax.ppermute(send, "core", swap)
    out = add_across(scalars, queries, partial, mine, 2, scale)
    return add_across(scalars, queries, partial, rest, 4, scale, before=out)


def solution(mesh):
    outer, inner = mesh.shape["outer"], mesh.shape["inner"]
    chips = Mesh(np.asarray(mesh.devices).reshape(outer, inner // 2, 2), ("outer", "z", "core"))
    everywhere = ("outer", "z", "core")
    return jax.shard_map(
        shards,
        mesh=chips,
        in_specs=(P(None, everywhere, None),) * 3 + (P(everywhere),) * 2,
        out_specs=P(None, everywhere, None),
        check_vma=False,
    )
```

```python
import functools
import math

import jax
import jax.numpy as jnp
import numpy as np
from jax import lax
from jax.experimental import pallas as pl
from jax.experimental.pallas import tpu as pltpu
from jax.sharding import Mesh
from jax.sharding import PartitionSpec as P

CHUNK = 256
MIB = 1 << 20
MARKS = 16


def rows_of(first, shape):
    return first + lax.broadcasted_iota(jnp.int32, shape, 0)


def in_hbm(x):
    return pltpu.with_memory_space_constraint(x, pltpu.HBM)


def in_vmem(x):
    return pltpu.with_memory_space_constraint(x, pltpu.VMEM)


def half_of(other):
    core = lax.axis_index("core")
    return 1 - core if other else core


SCALAR = pl.BlockSpec(memory_space=pltpu.SMEM)
WHOLE = pl.BlockSpec(memory_space=pltpu.VMEM)
ANYWHERE = pl.BlockSpec(memory_space=pl.ANY)


def state_kernel(heads, start_ref, k_ref, v_ref, s_ref, mask_ref):
    step = pl.program_id(0)
    length, width = k_ref.shape[1], k_ref.shape[2]

    @pl.when(step == 0)
    def _():
        start = start_ref[0]
        begin = jnp.where(start < length, start, 0)
        kept = rows_of(0, (length, width)) >= begin
        mask_ref[...] = jnp.where(kept, 1.0, 0.0).astype(mask_ref.dtype)
        reset = jnp.where(start < length, 1.0, 0.0)
        first = jnp.where(lax.axis_index("core") == 0, 1.0, 0.0)
        s_ref[-16:-8, :] = jnp.full((8, width), reset, jnp.float32)
        s_ref[-8:, :] = jnp.full((8, width), first, jnp.float32)

    for h in range(heads):
        state = lax.dot_general(
            k_ref[h] * mask_ref[...],
            v_ref[h],
            (((0,), (0,)), ((), ())),
            preferred_element_type=jnp.float32,
        )
        first = pl.multiple_of((step * heads + h) * width, width)
        s_ref[pl.ds(first, width), :] = state


def block_states(starts, keys, values, other, heads=2):
    count, length, width = keys.shape
    steps = count // 2 // heads
    spec = pl.BlockSpec((heads, length, width), lambda i: (half_of(other) * steps + i, 0, 0))
    rows = count // 2 * width + MARKS
    return pl.pallas_call(
        functools.partial(state_kernel, heads),
        out_shape=pltpu.VMEM((rows, width), jnp.float32),
        grid=(steps,),
        in_specs=[SCALAR, spec, spec],
        out_specs=pl.BlockSpec((rows, width), lambda i: (0, 0)),
        scratch_shapes=[pltpu.VMEM((length, width), jnp.bfloat16)],
        compiler_params=pltpu.CompilerParams(vmem_limit_bytes=12 * MIB),
        cost_estimate=pl.CostEstimate(
            flops=count * length * width * width,
            bytes_accessed=count * length * width * 2,
            transcendentals=0,
        ),
        name="states",
    )(starts, in_hbm(keys), in_hbm(values))


def marks(ref):
    return ref[-16:-8, :], ref[-8:, :]


def tiles(x):
    return x.reshape(x.shape[0] // 8, 8, x.shape[1])


def chip_kernel(own_ref, got_ref, out_ref):
    own_reset, first = marks(own_ref)
    got_reset, _ = marks(got_ref)
    own_part = 1.0 - first * got_reset
    got_part = 1.0 - (1.0 - first) * own_reset
    slices, rows, width = out_ref.shape
    data = slices * (rows - 8)
    total = tiles(own_ref[:data, :]) * own_part[None] + tiles(got_ref[:data, :]) * got_part[None]
    out_ref[:, : rows - 8, :] = total.reshape(slices, rows - 8, width)
    mark = jnp.maximum(got_reset, own_reset)
    out_ref[:, rows - 8 :, :] = jnp.broadcast_to(mark[None], (slices, 8, width))


def chip_states(own, got, slices):
    rows, width = own.shape
    return pl.pallas_call(
        chip_kernel,
        out_shape=pltpu.VMEM((slices, (rows - MARKS) // slices + 8, width), jnp.float32),
        in_specs=[WHOLE, WHOLE],
        out_specs=WHOLE,
        compiler_params=pltpu.CompilerParams(vmem_limit_bytes=8 * MIB),
        name="chip_states",
    )(in_vmem(own), in_vmem(got))


def scan_kernel(part_ref, after_ref, out_ref):
    slices, data, width = out_ref.shape

    def turn(c, before):
        out_ref[c] = before
        part = part_ref[c]
        kept = tiles(before) * (1.0 - part[data:, :])[None]
        return kept.reshape(data, width) + part[:data, :]

    lax.fori_loop(0, slices, turn, jnp.zeros((data, width), jnp.float32), unroll=8)


def scan_chips(parts, after):
    slices, rows, width = parts.shape
    return pl.pallas_call(
        scan_kernel,
        out_shape=pltpu.VMEM((slices, rows - 8, width), jnp.float32),
        in_specs=[WHOLE, ANYWHERE],
        out_specs=WHOLE,
        compiler_params=pltpu.CompilerParams(vmem_limit_bytes=8 * MIB),
        name="scan_chips",
    )(in_vmem(parts), after)


def send_kernel(before_ref, own_ref, out_ref):
    reset, first = marks(own_ref)
    data, width = out_ref.shape
    kept, added = 1.0 - first * reset, first
    total = tiles(before_ref[...]) * kept[None] + tiles(own_ref[:data, :]) * added[None]
    out_ref[...] = total.reshape(data, width)


def carried_to_send(before, own):
    return pl.pallas_call(
        send_kernel,
        out_shape=pltpu.VMEM(before.shape, jnp.float32),
        in_specs=[WHOLE, WHOLE],
        out_specs=WHOLE,
        compiler_params=pltpu.CompilerParams(vmem_limit_bytes=8 * MIB),
        name="carried_to_send",
    )(in_vmem(before), in_vmem(own))


def inside_kernel(
    heads,
    scale,
    start_ref,
    length_ref,
    q_ref,
    k_ref,
    v_ref,
    o_ref,
    weight_ref,
    token_ref,
    pair_ref,
    query_ref,
    key_ref,
    root_ref,
):
    start, length = start_ref[0], length_ref[0]
    rows, width = q_ref.shape[1], q_ref.shape[2]
    chunks = rows // CHUNK

    @pl.when(pl.program_id(0) == 0)
    def _():
        offsets = rows_of(0, (rows, width))
        counts = jnp.where(offsets < start, length + offsets + 1, offsets - start + 1)
        root = 1.0 / jnp.sqrt(counts.astype(jnp.float32))
        root_ref[...] = root
        weight_ref[...] = jnp.where(offsets < start, root * scale, 0.0)
        token_ref[...] = jnp.zeros_like(token_ref)
        for i in range(chunks):
            low = i * CHUNK
            inner = (start >= low) & (start < low + CHUNK)
            t = rows_of(low, (CHUNK, CHUNK))
            s = low + lax.broadcasted_iota(jnp.int32, (CHUNK, CHUNK), 1)
            allowed = (s <= t) & ((t < start) == (s < start))
            pair_ref[i] = jnp.where(allowed, scale, 0.0)
            t = rows_of(low, (CHUNK, width))
            cut = jnp.where(inner, start, low + CHUNK)
            query_ref[i] = jnp.where(t < cut, 1.0, 0.0)
            begin = jnp.where(inner, start, low)
            key_ref[i] = jnp.where(t >= begin, 1.0, 0.0).astype(key_ref.dtype)

    for h in range(heads):
        state = None
        for i in range(chunks):
            low = i * CHUNK
            here = slice(low, low + CHUNK)
            q, k, v = q_ref[h, here, :], k_ref[h, here, :], v_ref[h, here, :]
            scores = lax.dot_general(
                q, k, (((1,), (1,)), ((), ())), preferred_element_type=jnp.float32
            )
            scores = (scores * pair_ref[i]).astype(jnp.bfloat16)
            total = jnp.dot(scores, v, preferred_element_type=jnp.float32)
            if i > 0:
                past = (state * scale).astype(jnp.bfloat16)
                total += jnp.dot(q, past, preferred_element_type=jnp.float32) * query_ref[i]
            o_ref[h, here, :] = (total * root_ref[here, :]).astype(o_ref.dtype)
            if i < chunks - 1:
                new = lax.dot_general(
                    k * key_ref[i],
                    v,
                    (((0,), (0,)), ((), ())),
                    preferred_element_type=jnp.float32,
                )
                inner = (start >= low) & (start < low + CHUNK)
                state = new if i == 0 else new + state * jnp.where(inner, 0.0, 1.0)


def inside(starts, lengths, queries, keys, values, scale, heads=2):
    count, rows, width = queries.shape
    chunks = rows // CHUNK
    steps = count // heads
    spec = pl.BlockSpec((heads, rows, width), lambda i: (i, 0, 0))
    return pl.pallas_call(
        functools.partial(inside_kernel, heads, scale),
        out_shape=(
            jax.ShapeDtypeStruct((count, rows, width), jnp.bfloat16),
            jax.ShapeDtypeStruct((rows, width), jnp.float32),
            jax.ShapeDtypeStruct((8, width), jnp.float32),
        ),
        grid=(steps,),
        in_specs=[SCALAR, SCALAR, spec, spec, spec],
        out_specs=(
            spec,
            pl.BlockSpec((rows, width), lambda i: (0, 0)),
            pl.BlockSpec((8, width), lambda i: (0, 0)),
        ),
        scratch_shapes=[
            pltpu.VMEM((chunks, CHUNK, CHUNK), jnp.float32),
            pltpu.VMEM((chunks, CHUNK, width), jnp.float32),
            pltpu.VMEM((chunks, CHUNK, width), jnp.bfloat16),
            pltpu.VMEM((rows, width), jnp.float32),
        ],
        compiler_params=pltpu.CompilerParams(vmem_limit_bytes=16 * MIB),
        cost_estimate=pl.CostEstimate(
            flops=count * rows * width * (4 * CHUNK + 4 * width),
            bytes_accessed=count * rows * width * 8,
            transcendentals=0,
        ),
        name="inside",
    )(starts, lengths, in_hbm(queries), in_hbm(keys), in_hbm(values))


def final_kernel(other, heads, *refs):
    if other:
        q_ref, o_ref, w_ref, carried_ref, _, out_ref = refs
    else:
        q_ref, o_ref, w_ref, before_ref, got_ref, out_ref = refs
        reset, mate = marks(got_ref)
        kept, added = 1.0 - mate * reset, mate
    width = q_ref.shape[2]
    step = pl.program_id(0)
    nothing = jnp.zeros((width, width), jnp.bfloat16)

    def carried(h):
        first = pl.multiple_of((step * heads + h) * width, width)
        here = pl.ds(first, width)
        if other:
            return carried_ref[here, :].astype(jnp.bfloat16)
        total = tiles(before_ref[here, :]) * kept[None] + tiles(got_ref[here, :]) * added[None]
        return total.reshape(width, width).astype(jnp.bfloat16)

    for h in range(0, heads, 2):
        both = jnp.concatenate(
            [
                jnp.concatenate([carried(h), nothing], axis=1),
                jnp.concatenate([nothing, carried(h + 1)], axis=1),
            ],
            axis=0,
        )
        pair = jnp.concatenate([q_ref[h], q_ref[h + 1]], axis=1)
        across = jnp.dot(pair, both, preferred_element_type=jnp.float32)
        for k in range(2):
            part = across[:, k * width : (k + 1) * width]
            total = o_ref[h + k].astype(jnp.float32) + part * w_ref[...]
            out_ref[h + k] = total.astype(out_ref.dtype)


def finish(queries, partial, weights, carried, other, extra, heads=2):
    count, rows, width = queries.shape
    half = count // 2
    steps = half // heads
    spec = pl.BlockSpec((heads, rows, width), lambda i: (half_of(other) * steps + i, 0, 0))

    def all_of(x):
        return pl.BlockSpec(x.shape, lambda i: (0,) * x.ndim)

    return pl.pallas_call(
        functools.partial(final_kernel, other, heads),
        out_shape=jax.ShapeDtypeStruct(queries.shape, jnp.bfloat16),
        grid=(steps,),
        in_specs=[
            spec,
            spec,
            all_of(weights),
            all_of(carried),
            ANYWHERE if other else all_of(extra),
        ],
        out_specs=spec,
        input_output_aliases={4: 0} if other else {},
        compiler_params=pltpu.CompilerParams(vmem_limit_bytes=16 * MIB),
        cost_estimate=pl.CostEstimate(
            flops=2 * half * rows * width * width,
            bytes_accessed=half * rows * width * 6,
            transcendentals=0,
        ),
        name="finish",
    )(in_hbm(queries), in_hbm(partial), weights, carried, extra)


def shards(queries, keys, values, starts, lengths):
    width = queries.shape[2]
    scale = 1.0 / math.sqrt(width)
    chips = lax.axis_size("outer") * lax.axis_size("z")
    swap = [(0, 1), (1, 0)]

    theirs = block_states(starts, keys, values, True)
    got = lax.ppermute(theirs, "core", swap)
    own = block_states(starts, keys, values, False)
    parts = chip_states(own, got, chips)
    parts = lax.all_to_all(parts, ("outer", "z"), 0, 0, tiled=True)
    partial, weights, done = inside(starts, lengths, queries, keys, values, scale)
    befores = scan_chips(parts, done)
    before = lax.all_to_all(befores, ("outer", "z"), 0, 0, tiled=True)
    before = before.reshape(-1, width)
    send = carried_to_send(before, own)
    carried = lax.ppermute(send, "core", swap)
    out = finish(queries, partial, weights, before, False, got)
    return finish(queries, partial, weights, carried, True, out)


def solution(mesh):
    outer, inner = mesh.shape["outer"], mesh.shape["inner"]
    chips = Mesh(np.asarray(mesh.devices).reshape(outer, inner // 2, 2), ("outer", "z", "core"))
    everywhere = ("outer", "z", "core")
    return jax.shard_map(
        shards,
        mesh=chips,
        in_specs=(P(None, everywhere, None),) * 3 + (P(everywhere),) * 2,
        out_specs=P(None, everywhere, None),
        check_vma=False,
    )
```

```python
import functools
import math

import jax
import jax.numpy as jnp
import numpy as np
from jax import lax
from jax.experimental import pallas as pl
from jax.experimental.pallas import tpu as pltpu
from jax.sharding import Mesh
from jax.sharding import PartitionSpec as P

CHUNK = 256
MIB = 1 << 20
PIECES = 4
MARKS = 16


def rows_of(first, shape):
    return first + lax.broadcasted_iota(jnp.int32, shape, 0)


def in_hbm(x):
    return pltpu.with_memory_space_constraint(x, pltpu.HBM)


def in_vmem(x):
    return pltpu.with_memory_space_constraint(x, pltpu.VMEM)


def half_of(other):
    core = lax.axis_index("core")
    return 1 - core if other else core


def grouped(count, size):
    return [range(h, min(h + size, count)) for h in range(0, count, size)]


SCALAR = pl.BlockSpec(memory_space=pltpu.SMEM)
WHOLE = pl.BlockSpec(memory_space=pltpu.VMEM)
ANYWHERE = pl.BlockSpec(memory_space=pl.ANY)


def state_kernel(other, start_ref, k_hbm, v_hbm, s_ref, k_ref, v_ref, mask_ref, k_sems, v_sems):
    half, length, width = k_ref.shape
    base = half_of(other) * half
    copies = []
    for h in range(half):
        pair = (
            pltpu.make_async_copy(k_hbm.at[base + h], k_ref.at[h], k_sems.at[h]),
            pltpu.make_async_copy(v_hbm.at[base + h], v_ref.at[h], v_sems.at[h]),
        )
        for copy in pair:
            copy.start()
        copies.append(pair)
    start = start_ref[0]
    begin = jnp.where(start < length, start, 0)
    kept = rows_of(0, (length, width)) >= begin
    mask_ref[...] = jnp.where(kept, 1.0, 0.0).astype(mask_ref.dtype)
    reset = jnp.where(start < length, 1.0, 0.0)
    first = jnp.where(lax.axis_index("core") == 0, 1.0, 0.0)
    s_ref[-16:-8, :] = jnp.full((8, width), reset, jnp.float32)
    s_ref[-8:, :] = jnp.full((8, width), first, jnp.float32)
    for group in grouped(half, 3):
        for h in group:
            for copy in copies[h]:
                copy.wait()
        for h in group:
            s_ref[h * width : (h + 1) * width, :] = jnp.dot(
                k_ref[h].T, v_ref[h] * mask_ref[...], preferred_element_type=jnp.float32
            )


def block_states(starts, keys, values, other):
    count, length, width = keys.shape
    half = count // 2
    rows = half * width + MARKS
    return pl.pallas_call(
        functools.partial(state_kernel, other),
        out_shape=pltpu.VMEM((rows, width), jnp.float32),
        in_specs=[SCALAR, ANYWHERE, ANYWHERE],
        out_specs=WHOLE,
        scratch_shapes=[
            pltpu.VMEM((half, length, width), jnp.bfloat16),
            pltpu.VMEM((half, length, width), jnp.bfloat16),
            pltpu.VMEM((length, width), jnp.bfloat16),
            pltpu.SemaphoreType.DMA((half,)),
            pltpu.SemaphoreType.DMA((half,)),
        ],
        compiler_params=pltpu.CompilerParams(vmem_limit_bytes=16 * MIB),
        cost_estimate=pl.CostEstimate(
            flops=count * length * width * width,
            bytes_accessed=count * length * width * 2,
            transcendentals=0,
        ),
        name="states",
    )(starts, in_hbm(keys), in_hbm(values))


def marks(ref):
    return ref[-16:-8, :], ref[-8:, :]


def tiles(x):
    return x.reshape(x.shape[0] // 8, 8, x.shape[1])


def chip_kernel(own_ref, got_ref, out_hbm, out_ref, sems):
    own_reset, first = marks(own_ref)
    got_reset, _ = marks(got_ref)
    own_part = 1.0 - first * got_reset
    got_part = 1.0 - (1.0 - first) * own_reset
    mark = jnp.maximum(got_reset, own_reset)
    slices, rows, width = out_ref.shape
    data = rows - 8
    group = slices // PIECES
    copies = []
    for n in range(PIECES):
        here = slice(n * group * data, (n + 1) * group * data)
        there = slice(n * group, (n + 1) * group)
        total = tiles(own_ref[here, :]) * own_part[None] + tiles(got_ref[here, :]) * got_part[None]
        out_ref[there, :data, :] = total.reshape(group, data, width)
        out_ref[there, data:, :] = jnp.broadcast_to(mark[None], (group, 8, width))
        copy = pltpu.make_async_copy(out_ref.at[there], out_hbm.at[there], sems.at[n])
        copy.start()
        copies.append(copy)
    for copy in copies:
        copy.wait()


def chip_states(own, got, slices):
    rows, width = own.shape
    shape = (slices, (rows - MARKS) // slices + 8, width)
    return pl.pallas_call(
        chip_kernel,
        out_shape=pltpu.HBM(shape, jnp.float32),
        in_specs=[WHOLE, WHOLE],
        out_specs=ANYWHERE,
        scratch_shapes=[pltpu.VMEM(shape, jnp.float32), pltpu.SemaphoreType.DMA((PIECES,))],
        compiler_params=pltpu.CompilerParams(vmem_limit_bytes=8 * MIB),
        name="chip_states",
    )(in_vmem(own), in_vmem(got))


def scan_kernel(part_ref, after_ref, out_hbm, out_ref, sems):
    slices, data, width = out_ref.shape
    group = slices // PIECES
    before = jnp.zeros((data, width), jnp.float32)
    copies = []
    for n in range(PIECES):

        def turn(c, before, n=n):
            out_ref[n * group + c] = before
            part = part_ref[n * group + c]
            kept = tiles(before) * (1.0 - part[data:, :])[None]
            return kept.reshape(data, width) + part[:data, :]

        before = lax.fori_loop(0, group, turn, before, unroll=8)
        there = slice(n * group, (n + 1) * group)
        copy = pltpu.make_async_copy(out_ref.at[there], out_hbm.at[there], sems.at[n])
        copy.start()
        copies.append(copy)
    for copy in copies:
        copy.wait()


def scan_chips(parts, after):
    slices, rows, width = parts.shape
    shape = (slices, rows - 8, width)
    return pl.pallas_call(
        scan_kernel,
        out_shape=pltpu.HBM(shape, jnp.float32),
        in_specs=[WHOLE, ANYWHERE],
        out_specs=ANYWHERE,
        scratch_shapes=[pltpu.VMEM(shape, jnp.float32), pltpu.SemaphoreType.DMA((PIECES,))],
        compiler_params=pltpu.CompilerParams(vmem_limit_bytes=8 * MIB),
        name="scan_chips",
    )(in_vmem(parts), after)


def send_kernel(before_ref, own_ref, after_ref, out_ref):
    reset, first = marks(own_ref)
    data, width = out_ref.shape
    kept, added = 1.0 - first * reset, first
    total = tiles(before_ref[...]) * kept[None] + tiles(own_ref[:data, :]) * added[None]
    out_ref[...] = total.reshape(data, width)


def carried_to_send(before, own, after):
    return pl.pallas_call(
        send_kernel,
        out_shape=pltpu.VMEM(before.shape, jnp.float32),
        in_specs=[WHOLE, WHOLE, ANYWHERE],
        out_specs=WHOLE,
        compiler_params=pltpu.CompilerParams(vmem_limit_bytes=8 * MIB),
        name="carried_to_send",
    )(in_vmem(before), in_vmem(own), after)


def inside_kernel(
    heads,
    scale,
    start_ref,
    length_ref,
    q_ref,
    k_ref,
    v_ref,
    o_ref,
    weight_ref,
    token_ref,
    pair_ref,
    query_ref,
    key_ref,
    root_ref,
):
    rows, width = q_ref.shape[1], q_ref.shape[2]
    chunks = rows // CHUNK

    @pl.when(pl.program_id(0) == 0)
    def _():
        start, length = start_ref[0], length_ref[0]
        offsets = rows_of(0, (rows, width))
        counts = jnp.where(offsets < start, length + offsets + 1, offsets - start + 1)
        root = 1.0 / jnp.sqrt(counts.astype(jnp.float32))
        root_ref[...] = root
        weight_ref[...] = jnp.where(offsets < start, root * scale, 0.0)
        token_ref[...] = jnp.zeros_like(token_ref)
        for i in range(chunks):
            low = i * CHUNK
            inner = (start >= low) & (start < low + CHUNK)
            t = rows_of(low, (CHUNK, CHUNK))
            s = low + lax.broadcasted_iota(jnp.int32, (CHUNK, CHUNK), 1)
            allowed = (s <= t) & ((t < start) == (s < start))
            pair_ref[i] = jnp.where(allowed, scale, 0.0)
            t = rows_of(low, (CHUNK, width))
            cut = jnp.where(inner, start, low + CHUNK)
            query_ref[i] = jnp.where(t < cut, 1.0, 0.0)
            begin = jnp.where(inner, start, low)
            key_ref[i] = jnp.where(t >= begin, 1.0, 0.0).astype(key_ref.dtype)

    start = start_ref[0]
    for h in range(heads):
        state = None
        for i in range(chunks):
            low = i * CHUNK
            here = slice(low, low + CHUNK)
            q, k, v = q_ref[h, here, :], k_ref[h, here, :], v_ref[h, here, :]
            scores = lax.dot_general(
                q, k, (((1,), (1,)), ((), ())), preferred_element_type=jnp.float32
            )
            scores = (scores * pair_ref[i]).astype(jnp.bfloat16)
            total = jnp.dot(scores, v, preferred_element_type=jnp.float32)
            if i > 0:
                past = (state * scale).astype(jnp.bfloat16)
                total += jnp.dot(q, past, preferred_element_type=jnp.float32) * query_ref[i]
            o_ref[h, here, :] = (total * root_ref[here, :]).astype(o_ref.dtype)
            if i < chunks - 1:
                new = lax.dot_general(
                    k * key_ref[i],
                    v,
                    (((0,), (0,)), ((), ())),
                    preferred_element_type=jnp.float32,
                )
                inner = (start >= low) & (start < low + CHUNK)
                state = new if i == 0 else new + state * jnp.where(inner, 0.0, 1.0)


def inside(starts, lengths, queries, keys, values, scale, other, heads=2):
    count, rows, width = queries.shape
    chunks = rows // CHUNK
    half = count // 2
    steps = half // heads
    given = pl.BlockSpec((heads, rows, width), lambda i: (half_of(other) * steps + i, 0, 0))
    return pl.pallas_call(
        functools.partial(inside_kernel, heads, scale),
        out_shape=(
            pltpu.HBM((half, rows, width), jnp.bfloat16),
            jax.ShapeDtypeStruct((rows, width), jnp.float32),
            jax.ShapeDtypeStruct((8, width), jnp.float32),
        ),
        grid=(steps,),
        in_specs=[SCALAR, SCALAR, given, given, given],
        out_specs=(
            pl.BlockSpec((heads, rows, width), lambda i: (i, 0, 0)),
            pl.BlockSpec((rows, width), lambda i: (0, 0)),
            pl.BlockSpec((8, width), lambda i: (0, 0)),
        ),
        scratch_shapes=[
            pltpu.VMEM((chunks, CHUNK, CHUNK), jnp.float32),
            pltpu.VMEM((chunks, CHUNK, width), jnp.float32),
            pltpu.VMEM((chunks, CHUNK, width), jnp.bfloat16),
            pltpu.VMEM((rows, width), jnp.float32),
        ],
        compiler_params=pltpu.CompilerParams(vmem_limit_bytes=16 * MIB),
        cost_estimate=pl.CostEstimate(
            flops=half * rows * width * (4 * CHUNK + 4 * width),
            bytes_accessed=half * rows * width * 8,
            transcendentals=0,
        ),
        name="inside",
    )(starts, lengths, in_hbm(queries), in_hbm(keys), in_hbm(values))


def final_kernel(other, q_hbm, o_hbm, w_ref, carried_ref, *refs):
    if other:
        _, out_hbm, q_ref, o_ref, made_ref, q_sems, o_sems, out_sems = refs
    else:
        got_ref, out_hbm, q_ref, o_ref, made_ref, q_sems, o_sems, out_sems = refs
        reset, mate = marks(got_ref)
        kept, added = 1.0 - mate * reset, mate
    half, rows, width = q_ref.shape
    base = half_of(other) * half
    loads, stores = [], []
    for h in range(half):
        pair = (
            pltpu.make_async_copy(q_hbm.at[base + h], q_ref.at[h], q_sems.at[h]),
            pltpu.make_async_copy(o_hbm.at[h], o_ref.at[h], o_sems.at[h]),
        )
        for copy in pair:
            copy.start()
        loads.append(pair)
    nothing = jnp.zeros((width, width), jnp.bfloat16)

    def carried(h):
        here = slice(h * width, (h + 1) * width)
        total = carried_ref[here, :]
        if not other:
            total = tiles(total) * kept[None] + tiles(got_ref[here, :]) * added[None]
        return total.reshape(width, width).astype(jnp.bfloat16)

    for group in grouped(half, 4):
        for h in group:
            for copy in loads[h]:
                copy.wait()
        for h in group[::2]:
            both = jnp.concatenate(
                [
                    jnp.concatenate([carried(h), nothing], axis=1),
                    jnp.concatenate([nothing, carried(h + 1)], axis=1),
                ],
                axis=0,
            )
            pair = jnp.concatenate([q_ref[h], q_ref[h + 1]], axis=1)
            across = jnp.dot(pair, both, preferred_element_type=jnp.float32)
            for k in range(2):
                part = across[:, k * width : (k + 1) * width]
                total = o_ref[h + k].astype(jnp.float32) + part * w_ref[...]
                made_ref[h + k] = total.astype(made_ref.dtype)
        for h in group:
            store = pltpu.make_async_copy(made_ref.at[h], out_hbm.at[base + h], out_sems.at[h])
            store.start()
            stores.append(store)
    for store in stores:
        store.wait()


def finish(queries, partial, weights, carried, other, extra):
    count, rows, width = queries.shape
    half = count // 2
    return pl.pallas_call(
        functools.partial(final_kernel, other),
        out_shape=pltpu.HBM(queries.shape, jnp.bfloat16),
        in_specs=[ANYWHERE, ANYWHERE, WHOLE, WHOLE, ANYWHERE if other else WHOLE],
        out_specs=ANYWHERE,
        scratch_shapes=[pltpu.VMEM((half, rows, width), jnp.bfloat16)] * 3
        + [pltpu.SemaphoreType.DMA((half,))] * 3,
        input_output_aliases={4: 0} if other else {},
        compiler_params=pltpu.CompilerParams(vmem_limit_bytes=16 * MIB),
        cost_estimate=pl.CostEstimate(
            flops=2 * half * rows * width * width,
            bytes_accessed=half * rows * width * 6,
            transcendentals=0,
        ),
        name="finish",
    )(
        in_hbm(queries),
        in_hbm(partial),
        in_vmem(weights),
        in_vmem(carried),
        in_hbm(extra) if other else in_vmem(extra),
    )


def shards(queries, keys, values, starts, lengths):
    width = queries.shape[2]
    scale = 1.0 / math.sqrt(width)
    chips = lax.axis_size("outer") * lax.axis_size("z")
    swap = [(0, 1), (1, 0)]

    theirs = block_states(starts, keys, values, True)
    got = lax.ppermute(theirs, "core", swap)
    own = block_states(starts, keys, values, False)
    parts = chip_states(own, got, chips)
    parts = lax.all_to_all(parts, ("outer", "z"), 0, 0, tiled=True)
    mine, weights, done = inside(starts, lengths, queries, keys, values, scale, False)
    befores = scan_chips(parts, done)
    before = lax.all_to_all(befores, ("outer", "z"), 0, 0, tiled=True)
    rest, _, done = inside(starts, lengths, queries, keys, values, scale, True)
    before = before.reshape(-1, width)
    send = carried_to_send(before, own, done)
    carried = lax.ppermute(send, "core", swap)
    out = finish(queries, mine, weights, before, False, got)
    return finish(queries, rest, weights, carried, True, out)


def solution(mesh):
    outer, inner = mesh.shape["outer"], mesh.shape["inner"]
    chips = Mesh(np.asarray(mesh.devices).reshape(outer, inner // 2, 2), ("outer", "z", "core"))
    everywhere = ("outer", "z", "core")
    return jax.shard_map(
        shards,
        mesh=chips,
        in_specs=(P(None, everywhere, None),) * 3 + (P(everywhere),) * 2,
        out_specs=P(None, everywhere, None),
        check_vma=False,
    )
```

```python
import functools
import math

import jax
import jax.numpy as jnp
import numpy as np
from jax import lax
from jax.experimental import pallas as pl
from jax.experimental.pallas import tpu as pltpu
from jax.sharding import Mesh
from jax.sharding import PartitionSpec as P

CHUNK = 256
MIB = 1 << 20
PIECES = 4
MARKS = 16


def rows_of(first, shape):
    return first + lax.broadcasted_iota(jnp.int32, shape, 0)


def in_hbm(x):
    return pltpu.with_memory_space_constraint(x, pltpu.HBM)


def in_vmem(x):
    return pltpu.with_memory_space_constraint(x, pltpu.VMEM)


def half_of(other):
    core = lax.axis_index("core")
    return 1 - core if other else core


def grouped(count, size):
    return [range(h, min(h + size, count)) for h in range(0, count, size)]


SCALAR = pl.BlockSpec(memory_space=pltpu.SMEM)
WHOLE = pl.BlockSpec(memory_space=pltpu.VMEM)
ANYWHERE = pl.BlockSpec(memory_space=pl.ANY)


def state_kernel(other, start_ref, k_hbm, v_hbm, s_ref, k_ref, v_ref, mask_ref, k_sems, v_sems):
    half, length, width = k_ref.shape
    base = half_of(other) * half
    copies = []
    for h in range(half):
        pair = (
            pltpu.make_async_copy(k_hbm.at[base + h], k_ref.at[h], k_sems.at[h]),
            pltpu.make_async_copy(v_hbm.at[base + h], v_ref.at[h], v_sems.at[h]),
        )
        for copy in pair:
            copy.start()
        copies.append(pair)
    start = start_ref[0]
    begin = jnp.where(start < length, start, 0)
    kept = rows_of(0, (length, width)) >= begin
    mask_ref[...] = jnp.where(kept, 1.0, 0.0).astype(mask_ref.dtype)
    reset = jnp.where(start < length, 1.0, 0.0)
    first = jnp.where(lax.axis_index("core") == 0, 1.0, 0.0)
    s_ref[-16:-8, :] = jnp.full((8, width), reset, jnp.float32)
    s_ref[-8:, :] = jnp.full((8, width), first, jnp.float32)
    for group in grouped(half, 3):
        for h in group:
            for copy in copies[h]:
                copy.wait()
        for h in group:
            s_ref[h * width : (h + 1) * width, :] = jnp.dot(
                k_ref[h].T, v_ref[h] * mask_ref[...], preferred_element_type=jnp.float32
            )


def block_states(starts, keys, values, other):
    count, length, width = keys.shape
    half = count // 2
    rows = half * width + MARKS
    return pl.pallas_call(
        functools.partial(state_kernel, other),
        out_shape=pltpu.VMEM((rows, width), jnp.float32),
        in_specs=[SCALAR, ANYWHERE, ANYWHERE],
        out_specs=WHOLE,
        scratch_shapes=[
            pltpu.VMEM((half, length, width), jnp.bfloat16),
            pltpu.VMEM((half, length, width), jnp.bfloat16),
            pltpu.VMEM((length, width), jnp.bfloat16),
            pltpu.SemaphoreType.DMA((half,)),
            pltpu.SemaphoreType.DMA((half,)),
        ],
        compiler_params=pltpu.CompilerParams(vmem_limit_bytes=16 * MIB),
        cost_estimate=pl.CostEstimate(
            flops=count * length * width * width,
            bytes_accessed=count * length * width * 2,
            transcendentals=0,
        ),
        name="states",
    )(starts, in_hbm(keys), in_hbm(values))


def marks(ref):
    return ref[-16:-8, :], ref[-8:, :]


def tiles(x):
    return x.reshape(x.shape[0] // 8, 8, x.shape[1])


def chip_kernel(slices, own_ref, got_ref, out_hbm, out_ref, sems):
    own_reset, first = marks(own_ref)
    got_reset, _ = marks(got_ref)
    own_part = 1.0 - first * got_reset
    got_part = 1.0 - (1.0 - first) * own_reset
    mark = jnp.maximum(got_reset, own_reset)
    data = (own_ref.shape[0] - MARKS) // slices
    rows = data + 1
    group = slices // PIECES
    copies = []
    for n in range(PIECES):
        here = slice(n * group * data, (n + 1) * group * data)
        total = tiles(own_ref[here, :]) * own_part[None] + tiles(got_ref[here, :]) * got_part[None]
        total = total.reshape(group * data, -1)
        for p in range(group):
            first_row = (n * group + p) * rows
            out_ref[first_row : first_row + data, :] = total[p * data : (p + 1) * data, :]
            out_ref[first_row + data : first_row + rows, :] = mark[:1, :]
        there = slice(n * group * rows, (n + 1) * group * rows)
        copy = pltpu.make_async_copy(out_ref.at[there], out_hbm.at[there], sems.at[n])
        copy.start()
        copies.append(copy)
    for copy in copies:
        copy.wait()


def chip_states(own, got, slices):
    rows, width = own.shape
    shape = (rows - MARKS + slices, width)
    return pl.pallas_call(
        functools.partial(chip_kernel, slices),
        out_shape=pltpu.HBM(shape, jnp.float32),
        in_specs=[WHOLE, WHOLE],
        out_specs=ANYWHERE,
        scratch_shapes=[pltpu.VMEM(shape, jnp.float32), pltpu.SemaphoreType.DMA((PIECES,))],
        compiler_params=pltpu.CompilerParams(vmem_limit_bytes=8 * MIB),
        name="chip_states",
    )(in_vmem(own), in_vmem(got))


def scan_kernel(part_ref, after_ref, out_hbm, out_ref, sems):
    slices, data, width = out_ref.shape
    group = slices // PIECES
    before = jnp.zeros((data, width), jnp.float32)
    copies = []
    for n in range(PIECES):
        there = slice(n * group, (n + 1) * group)
        for c in range(slices)[there]:
            out_ref[c] = before
            first = c * (data + 1)
            reset = part_ref[first + data : first + data + 1, :]
            before = before * (1.0 - reset) + part_ref[first : first + data, :]
        copy = pltpu.make_async_copy(out_ref.at[there], out_hbm.at[there], sems.at[n])
        copy.start()
        copies.append(copy)
    for copy in copies:
        copy.wait()


def scan_chips(parts, after, slices):
    rows, width = parts.shape
    shape = (slices, rows // slices - 1, width)
    return pl.pallas_call(
        scan_kernel,
        out_shape=pltpu.HBM(shape, jnp.float32),
        in_specs=[WHOLE, ANYWHERE],
        out_specs=ANYWHERE,
        scratch_shapes=[pltpu.VMEM(shape, jnp.float32), pltpu.SemaphoreType.DMA((PIECES,))],
        compiler_params=pltpu.CompilerParams(vmem_limit_bytes=8 * MIB),
        name="scan_chips",
    )(in_vmem(parts), after)


def send_kernel(before_ref, own_ref, after_ref, out_ref):
    reset, first = marks(own_ref)
    data, width = out_ref.shape
    kept, added = 1.0 - first * reset, first
    total = tiles(before_ref[...]) * kept[None] + tiles(own_ref[:data, :]) * added[None]
    out_ref[...] = total.reshape(data, width)


def carried_to_send(before, own, after):
    return pl.pallas_call(
        send_kernel,
        out_shape=pltpu.VMEM(before.shape, jnp.float32),
        in_specs=[WHOLE, WHOLE, ANYWHERE],
        out_specs=WHOLE,
        compiler_params=pltpu.CompilerParams(vmem_limit_bytes=8 * MIB),
        name="carried_to_send",
    )(in_vmem(before), in_vmem(own), after)


def inside_kernel(
    heads,
    scale,
    start_ref,
    length_ref,
    q_ref,
    k_ref,
    v_ref,
    o_ref,
    weight_ref,
    token_ref,
    pair_ref,
    query_ref,
    key_ref,
    root_ref,
):
    rows, width = q_ref.shape[1], q_ref.shape[2]
    chunks = rows // CHUNK

    @pl.when(pl.program_id(0) == 0)
    def _():
        start, length = start_ref[0], length_ref[0]
        offsets = rows_of(0, (rows, width))
        counts = jnp.where(offsets < start, length + offsets + 1, offsets - start + 1)
        root = 1.0 / jnp.sqrt(counts.astype(jnp.float32))
        root_ref[...] = root
        weight_ref[...] = jnp.where(offsets < start, root * scale, 0.0)
        token_ref[...] = jnp.zeros_like(token_ref)
        for i in range(chunks):
            low = i * CHUNK
            inner = (start >= low) & (start < low + CHUNK)
            t = rows_of(low, (CHUNK, CHUNK))
            s = low + lax.broadcasted_iota(jnp.int32, (CHUNK, CHUNK), 1)
            allowed = (s <= t) & ((t < start) == (s < start))
            pair_ref[i] = jnp.where(allowed, scale, 0.0)
            t = rows_of(low, (CHUNK, width))
            cut = jnp.where(inner, start, low + CHUNK)
            query_ref[i] = jnp.where(t < cut, 1.0, 0.0)
            begin = jnp.where(inner, start, low)
            key_ref[i] = jnp.where(t >= begin, 1.0, 0.0).astype(key_ref.dtype)

    start = start_ref[0]
    for h in range(heads):
        state = None
        for i in range(chunks):
            low = i * CHUNK
            here = slice(low, low + CHUNK)
            q, k, v = q_ref[h, here, :], k_ref[h, here, :], v_ref[h, here, :]
            scores = lax.dot_general(
                q, k, (((1,), (1,)), ((), ())), preferred_element_type=jnp.float32
            )
            scores = (scores * pair_ref[i]).astype(jnp.bfloat16)
            total = jnp.dot(scores, v, preferred_element_type=jnp.float32)
            if i > 0:
                past = (state * scale).astype(jnp.bfloat16)
                total += jnp.dot(q, past, preferred_element_type=jnp.float32) * query_ref[i]
            o_ref[h, here, :] = (total * root_ref[here, :]).astype(o_ref.dtype)
            if i < chunks - 1:
                new = lax.dot_general(
                    k * key_ref[i],
                    v,
                    (((0,), (0,)), ((), ())),
                    preferred_element_type=jnp.float32,
                )
                inner = (start >= low) & (start < low + CHUNK)
                state = new if i == 0 else new + state * jnp.where(inner, 0.0, 1.0)


def inside(starts, lengths, queries, keys, values, scale, other, heads=2):
    count, rows, width = queries.shape
    chunks = rows // CHUNK
    half = count // 2
    steps = half // heads
    given = pl.BlockSpec((heads, rows, width), lambda i: (half_of(other) * steps + i, 0, 0))
    return pl.pallas_call(
        functools.partial(inside_kernel, heads, scale),
        out_shape=(
            pltpu.HBM((half, rows, width), jnp.bfloat16),
            jax.ShapeDtypeStruct((rows, width), jnp.float32),
            jax.ShapeDtypeStruct((8, width), jnp.float32),
        ),
        grid=(steps,),
        in_specs=[SCALAR, SCALAR, given, given, given],
        out_specs=(
            pl.BlockSpec((heads, rows, width), lambda i: (i, 0, 0)),
            pl.BlockSpec((rows, width), lambda i: (0, 0)),
            pl.BlockSpec((8, width), lambda i: (0, 0)),
        ),
        scratch_shapes=[
            pltpu.VMEM((chunks, CHUNK, CHUNK), jnp.float32),
            pltpu.VMEM((chunks, CHUNK, width), jnp.float32),
            pltpu.VMEM((chunks, CHUNK, width), jnp.bfloat16),
            pltpu.VMEM((rows, width), jnp.float32),
        ],
        compiler_params=pltpu.CompilerParams(vmem_limit_bytes=16 * MIB),
        cost_estimate=pl.CostEstimate(
            flops=half * rows * width * (4 * CHUNK + 4 * width),
            bytes_accessed=half * rows * width * 8,
            transcendentals=0,
        ),
        name="inside",
    )(starts, lengths, in_hbm(queries), in_hbm(keys), in_hbm(values))


def final_kernel(other, q_hbm, o_hbm, w_ref, carried_ref, *refs):
    if other:
        _, out_hbm, q_ref, o_ref, made_ref, q_sems, o_sems, out_sems = refs
    else:
        got_ref, out_hbm, q_ref, o_ref, made_ref, q_sems, o_sems, out_sems = refs
        reset, mate = marks(got_ref)
        kept, added = 1.0 - mate * reset, mate
    half, rows, width = q_ref.shape
    base = half_of(other) * half
    loads, stores = [], []
    for h in range(half):
        pair = (
            pltpu.make_async_copy(q_hbm.at[base + h], q_ref.at[h], q_sems.at[h]),
            pltpu.make_async_copy(o_hbm.at[h], o_ref.at[h], o_sems.at[h]),
        )
        for copy in pair:
            copy.start()
        loads.append(pair)
    nothing = jnp.zeros((width, width), jnp.bfloat16)

    def carried(h):
        here = slice(h * width, (h + 1) * width)
        total = carried_ref[here, :]
        if not other:
            total = tiles(total) * kept[None] + tiles(got_ref[here, :]) * added[None]
        return total.reshape(width, width).astype(jnp.bfloat16)

    for group in grouped(half, 4)[:-1] + grouped(half, 2)[-2:]:
        for h in group:
            for copy in loads[h]:
                copy.wait()
        for h in group[::2]:
            both = jnp.concatenate(
                [
                    jnp.concatenate([carried(h), nothing], axis=1),
                    jnp.concatenate([nothing, carried(h + 1)], axis=1),
                ],
                axis=0,
            )
            pair = jnp.concatenate([q_ref[h], q_ref[h + 1]], axis=1)
            across = jnp.dot(pair, both, preferred_element_type=jnp.float32)
            for k in range(2):
                part = across[:, k * width : (k + 1) * width]
                total = o_ref[h + k].astype(jnp.float32) + part * w_ref[...]
                made_ref[h + k] = total.astype(made_ref.dtype)
        for h in group:
            store = pltpu.make_async_copy(made_ref.at[h], out_hbm.at[base + h], out_sems.at[h])
            store.start()
            stores.append(store)
    for store in stores:
        store.wait()


def finish(queries, partial, weights, carried, other, extra):
    count, rows, width = queries.shape
    half = count // 2
    return pl.pallas_call(
        functools.partial(final_kernel, other),
        out_shape=pltpu.HBM(queries.shape, jnp.bfloat16),
        in_specs=[ANYWHERE, ANYWHERE, WHOLE, WHOLE, ANYWHERE if other else WHOLE],
        out_specs=ANYWHERE,
        scratch_shapes=[pltpu.VMEM((half, rows, width), jnp.bfloat16)] * 3
        + [pltpu.SemaphoreType.DMA((half,))] * 3,
        input_output_aliases={4: 0} if other else {},
        compiler_params=pltpu.CompilerParams(vmem_limit_bytes=16 * MIB),
        cost_estimate=pl.CostEstimate(
            flops=2 * half * rows * width * width,
            bytes_accessed=half * rows * width * 6,
            transcendentals=0,
        ),
        name="finish",
    )(
        in_hbm(queries),
        in_hbm(partial),
        in_vmem(weights),
        in_vmem(carried),
        in_hbm(extra) if other else in_vmem(extra),
    )


def shards(queries, keys, values, starts, lengths):
    width = queries.shape[2]
    scale = 1.0 / math.sqrt(width)
    chips = lax.axis_size("outer") * lax.axis_size("z")
    swap = [(0, 1), (1, 0)]

    theirs = block_states(starts, keys, values, True)
    got = lax.ppermute(theirs, "core", swap)
    own = block_states(starts, keys, values, False)
    parts = chip_states(own, got, chips)
    parts = lax.all_to_all(parts.reshape(chips, 1, -1), ("outer", "z"), 0, 0, tiled=True)
    parts = parts.reshape(-1, width)
    mine, weights, done = inside(starts, lengths, queries, keys, values, scale, False)
    befores = scan_chips(parts, done, chips)
    before = lax.all_to_all(befores, ("outer", "z"), 0, 0, tiled=True)
    rest, _, done = inside(starts, lengths, queries, keys, values, scale, True)
    before = before.reshape(-1, width)
    send = carried_to_send(before, own, done)
    carried = lax.ppermute(send, "core", swap)
    out = finish(queries, mine, weights, before, False, got)
    return finish(queries, rest, weights, carried, True, out)


def solution(mesh):
    outer, inner = mesh.shape["outer"], mesh.shape["inner"]
    chips = Mesh(np.asarray(mesh.devices).reshape(outer, inner // 2, 2), ("outer", "z", "core"))
    everywhere = ("outer", "z", "core")
    return jax.shard_map(
        shards,
        mesh=chips,
        in_specs=(P(None, everywhere, None),) * 3 + (P(everywhere),) * 2,
        out_specs=P(None, everywhere, None),
        check_vma=False,
    )
```

```python
import functools
import math

import jax
import jax.numpy as jnp
import numpy as np
from jax import lax
from jax.experimental import pallas as pl
from jax.experimental.pallas import tpu as pltpu
from jax.sharding import Mesh
from jax.sharding import PartitionSpec as P

CHUNK = 256
MIB = 1 << 20
PIECES = 4
MARKS = 16


def rows_of(first, shape):
    return first + lax.broadcasted_iota(jnp.int32, shape, 0)


def in_hbm(x):
    return pltpu.with_memory_space_constraint(x, pltpu.HBM)


def in_vmem(x):
    return pltpu.with_memory_space_constraint(x, pltpu.VMEM)


def half_of(other):
    core = lax.axis_index("core")
    return 1 - core if other else core


def grouped(count, size):
    return [range(h, min(h + size, count)) for h in range(0, count, size)]


SCALAR = pl.BlockSpec(memory_space=pltpu.SMEM)
WHOLE = pl.BlockSpec(memory_space=pltpu.VMEM)
ANYWHERE = pl.BlockSpec(memory_space=pl.ANY)


def state_kernel(other, start_ref, k_hbm, v_hbm, s_ref, k_ref, v_ref, mask_ref, k_sems, v_sems):
    half, length, width = k_ref.shape
    base = half_of(other) * half
    copies = []
    for h in range(half):
        pair = (
            pltpu.make_async_copy(k_hbm.at[base + h], k_ref.at[h], k_sems.at[h]),
            pltpu.make_async_copy(v_hbm.at[base + h], v_ref.at[h], v_sems.at[h]),
        )
        for copy in pair:
            copy.start()
        copies.append(pair)
    start = start_ref[0]
    begin = jnp.where(start < length, start, 0)
    kept = rows_of(0, (length, width)) >= begin
    mask_ref[...] = jnp.where(kept, 1.0, 0.0).astype(mask_ref.dtype)
    reset = jnp.where(start < length, 1.0, 0.0)
    first = jnp.where(lax.axis_index("core") == 0, 1.0, 0.0)
    s_ref[-16:-8, :] = jnp.full((8, width), reset, jnp.float32)
    s_ref[-8:, :] = jnp.full((8, width), first, jnp.float32)
    for group in grouped(half, 3):
        for h in group:
            for copy in copies[h]:
                copy.wait()
        for h in group:
            s_ref[h * width : (h + 1) * width, :] = jnp.dot(
                k_ref[h].T, v_ref[h] * mask_ref[...], preferred_element_type=jnp.float32
            )


def block_states(starts, keys, values, other):
    count, length, width = keys.shape
    half = count // 2
    rows = half * width + MARKS
    return pl.pallas_call(
        functools.partial(state_kernel, other),
        out_shape=pltpu.VMEM((rows, width), jnp.float32),
        in_specs=[SCALAR, ANYWHERE, ANYWHERE],
        out_specs=WHOLE,
        scratch_shapes=[
            pltpu.VMEM((half, length, width), jnp.bfloat16),
            pltpu.VMEM((half, length, width), jnp.bfloat16),
            pltpu.VMEM((length, width), jnp.bfloat16),
            pltpu.SemaphoreType.DMA((half,)),
            pltpu.SemaphoreType.DMA((half,)),
        ],
        compiler_params=pltpu.CompilerParams(vmem_limit_bytes=16 * MIB),
        cost_estimate=pl.CostEstimate(
            flops=count * length * width * width,
            bytes_accessed=count * length * width * 2,
            transcendentals=0,
        ),
        name="states",
    )(starts, in_hbm(keys), in_hbm(values))


def marks(ref):
    return ref[-16:-8, :], ref[-8:, :]


def tiles(x):
    return x.reshape(x.shape[0] // 8, 8, x.shape[1])


def chip_kernel(slices, own_ref, got_ref, out_hbm, out_ref, sems):
    own_reset, first = marks(own_ref)
    got_reset, _ = marks(got_ref)
    own_part = 1.0 - first * got_reset
    got_part = 1.0 - (1.0 - first) * own_reset
    mark = jnp.maximum(got_reset, own_reset)
    data = (own_ref.shape[0] - MARKS) // slices
    rows = data + 1
    group = slices // PIECES
    copies = []
    for n in range(PIECES):
        here = slice(n * group * data, (n + 1) * group * data)
        total = tiles(own_ref[here, :]) * own_part[None] + tiles(got_ref[here, :]) * got_part[None]
        total = total.reshape(group * data, -1)
        for p in range(group):
            first_row = (n * group + p) * rows
            out_ref[first_row : first_row + data, :] = total[p * data : (p + 1) * data, :]
            out_ref[first_row + data : first_row + rows, :] = mark[:1, :]
        there = slice(n * group * rows, (n + 1) * group * rows)
        copy = pltpu.make_async_copy(out_ref.at[there], out_hbm.at[there], sems.at[n])
        copy.start()
        copies.append(copy)
    for copy in copies:
        copy.wait()


def chip_states(own, got, slices):
    rows, width = own.shape
    shape = (rows - MARKS + slices, width)
    return pl.pallas_call(
        functools.partial(chip_kernel, slices),
        out_shape=pltpu.HBM(shape, jnp.float32),
        in_specs=[WHOLE, WHOLE],
        out_specs=ANYWHERE,
        scratch_shapes=[pltpu.VMEM(shape, jnp.float32), pltpu.SemaphoreType.DMA((PIECES,))],
        compiler_params=pltpu.CompilerParams(vmem_limit_bytes=8 * MIB),
        name="chip_states",
    )(in_vmem(own), in_vmem(got))


def scan_kernel(part_ref, after_ref, out_hbm, out_ref, sems):
    slices, data, width = out_ref.shape
    group = slices // PIECES
    before = jnp.zeros((data, width), jnp.float32)
    copies = []
    for n in range(PIECES):
        there = slice(n * group, (n + 1) * group)
        for c in range(slices)[there]:
            out_ref[c] = before
            first = c * (data + 1)
            reset = part_ref[first + data : first + data + 1, :]
            before = before * (1.0 - reset) + part_ref[first : first + data, :]
        copy = pltpu.make_async_copy(out_ref.at[there], out_hbm.at[there], sems.at[n])
        copy.start()
        copies.append(copy)
    for copy in copies:
        copy.wait()


def scan_chips(parts, after, slices):
    rows, width = parts.shape
    shape = (slices, rows // slices - 1, width)
    return pl.pallas_call(
        scan_kernel,
        out_shape=pltpu.HBM(shape, jnp.float32),
        in_specs=[WHOLE, ANYWHERE],
        out_specs=ANYWHERE,
        scratch_shapes=[pltpu.VMEM(shape, jnp.float32), pltpu.SemaphoreType.DMA((PIECES,))],
        compiler_params=pltpu.CompilerParams(vmem_limit_bytes=8 * MIB),
        name="scan_chips",
    )(in_vmem(parts), after)


def send_kernel(before_ref, own_ref, after_ref, out_ref):
    reset, first = marks(own_ref)
    data, width = out_ref.shape
    kept, added = 1.0 - first * reset, first
    total = tiles(before_ref[...]) * kept[None] + tiles(own_ref[:data, :]) * added[None]
    out_ref[...] = total.reshape(data, width)


def carried_to_send(before, own, after):
    return pl.pallas_call(
        send_kernel,
        out_shape=pltpu.VMEM(before.shape, jnp.float32),
        in_specs=[WHOLE, WHOLE, ANYWHERE],
        out_specs=WHOLE,
        compiler_params=pltpu.CompilerParams(vmem_limit_bytes=8 * MIB),
        name="carried_to_send",
    )(in_vmem(before), in_vmem(own), after)


def inside_kernel(
    heads,
    scale,
    start_ref,
    length_ref,
    q_ref,
    k_ref,
    v_ref,
    o_ref,
    weight_ref,
    token_ref,
    pair_ref,
    query_ref,
    key_ref,
    root_ref,
):
    rows, width = q_ref.shape[1], q_ref.shape[2]
    chunks = rows // CHUNK

    @pl.when(pl.program_id(0) == 0)
    def _():
        start, length = start_ref[0], length_ref[0]
        offsets = rows_of(0, (rows, width))
        counts = jnp.where(offsets < start, length + offsets + 1, offsets - start + 1)
        root = 1.0 / jnp.sqrt(counts.astype(jnp.float32))
        root_ref[...] = root
        weight_ref[...] = jnp.where(offsets < start, root * scale, 0.0)
        token_ref[...] = jnp.zeros_like(token_ref)
        for i in range(chunks):
            low = i * CHUNK
            inner = (start >= low) & (start < low + CHUNK)
            t = rows_of(low, (CHUNK, CHUNK))
            s = low + lax.broadcasted_iota(jnp.int32, (CHUNK, CHUNK), 1)
            allowed = (s <= t) & ((t < start) == (s < start))
            pair_ref[i] = jnp.where(allowed, scale, 0.0)
            t = rows_of(low, (CHUNK, width))
            cut = jnp.where(inner, start, low + CHUNK)
            query_ref[i] = jnp.where(t < cut, 1.0, 0.0).astype(query_ref.dtype)
            begin = jnp.where(inner, start, low)
            key_ref[i] = jnp.where(t >= begin, 1.0, 0.0).astype(key_ref.dtype)

    start = start_ref[0]
    states = [None] * heads
    for i in range(chunks):
        low = i * CHUNK
        here = slice(low, low + CHUNK)
        inner = (start >= low) & (start < low + CHUNK)
        scores = []
        for h in range(heads):
            product = lax.dot_general(
                q_ref[h, here, :],
                k_ref[h, here, :],
                (((1,), (1,)), ((), ())),
                preferred_element_type=jnp.float32,
            )
            scores.append((product * pair_ref[i]).astype(jnp.bfloat16))
        for h in range(heads):
            q, k, v = q_ref[h, here, :], k_ref[h, here, :], v_ref[h, here, :]
            total = jnp.dot(scores[h], v, preferred_element_type=jnp.float32)
            if i > 0:
                past = (states[h] * scale).astype(jnp.bfloat16)
                masked = q * query_ref[i]
                total += jnp.dot(masked, past, preferred_element_type=jnp.float32)
            o_ref[h, here, :] = (total * root_ref[here, :]).astype(o_ref.dtype)
            if i < chunks - 1:
                new = jnp.dot(k.T, v * key_ref[i], preferred_element_type=jnp.float32)
                states[h] = new if i == 0 else new + states[h] * jnp.where(inner, 0.0, 1.0)


def inside(starts, lengths, queries, keys, values, scale, other, heads=4):
    count, rows, width = queries.shape
    chunks = rows // CHUNK
    half = count // 2
    steps = half // heads
    given = pl.BlockSpec((heads, rows, width), lambda i: (half_of(other) * steps + i, 0, 0))
    return pl.pallas_call(
        functools.partial(inside_kernel, heads, scale),
        out_shape=(
            pltpu.HBM((half, rows, width), jnp.bfloat16),
            jax.ShapeDtypeStruct((rows, width), jnp.float32),
            jax.ShapeDtypeStruct((8, width), jnp.float32),
        ),
        grid=(steps,),
        in_specs=[SCALAR, SCALAR, given, given, given],
        out_specs=(
            pl.BlockSpec((heads, rows, width), lambda i: (i, 0, 0)),
            pl.BlockSpec((rows, width), lambda i: (0, 0)),
            pl.BlockSpec((8, width), lambda i: (0, 0)),
        ),
        scratch_shapes=[
            pltpu.VMEM((chunks, CHUNK, CHUNK), jnp.float32),
            pltpu.VMEM((chunks, CHUNK, width), jnp.bfloat16),
            pltpu.VMEM((chunks, CHUNK, width), jnp.bfloat16),
            pltpu.VMEM((rows, width), jnp.float32),
        ],
        compiler_params=pltpu.CompilerParams(vmem_limit_bytes=24 * MIB),
        cost_estimate=pl.CostEstimate(
            flops=half * rows * width * (4 * CHUNK + 4 * width),
            bytes_accessed=half * rows * width * 8,
            transcendentals=0,
        ),
        name="inside",
    )(starts, lengths, in_hbm(queries), in_hbm(keys), in_hbm(values))


def final_kernel(other, q_hbm, o_hbm, w_ref, carried_ref, *refs):
    if other:
        _, out_hbm, q_ref, o_ref, made_ref, q_sems, o_sems, out_sems = refs
    else:
        got_ref, out_hbm, q_ref, o_ref, made_ref, q_sems, o_sems, out_sems = refs
        reset, mate = marks(got_ref)
        kept, added = 1.0 - mate * reset, mate
    half, rows, width = q_ref.shape
    base = half_of(other) * half
    loads, stores = [], []
    for h in range(half):
        pair = (
            pltpu.make_async_copy(q_hbm.at[base + h], q_ref.at[h], q_sems.at[h]),
            pltpu.make_async_copy(o_hbm.at[h], o_ref.at[h], o_sems.at[h]),
        )
        for copy in pair:
            copy.start()
        loads.append(pair)
    nothing = jnp.zeros((width, width), jnp.bfloat16)

    def carried(h):
        here = slice(h * width, (h + 1) * width)
        total = carried_ref[here, :]
        if not other:
            total = tiles(total) * kept[None] + tiles(got_ref[here, :]) * added[None]
        return total.reshape(width, width).astype(jnp.bfloat16)

    for group in grouped(half, 4)[:-1] + grouped(half, 2)[-2:]:
        for h in group:
            for copy in loads[h]:
                copy.wait()
        for h in group[::2]:
            both = jnp.concatenate(
                [
                    jnp.concatenate([carried(h), nothing], axis=1),
                    jnp.concatenate([nothing, carried(h + 1)], axis=1),
                ],
                axis=0,
            )
            pair = jnp.concatenate([q_ref[h], q_ref[h + 1]], axis=1)
            across = jnp.dot(pair, both, preferred_element_type=jnp.float32)
            for k in range(2):
                part = across[:, k * width : (k + 1) * width]
                total = o_ref[h + k].astype(jnp.float32) + part * w_ref[...]
                made_ref[h + k] = total.astype(made_ref.dtype)
        for h in group:
            store = pltpu.make_async_copy(made_ref.at[h], out_hbm.at[base + h], out_sems.at[h])
            store.start()
            stores.append(store)
    for store in stores:
        store.wait()


def finish(queries, partial, weights, carried, other, extra):
    count, rows, width = queries.shape
    half = count // 2
    return pl.pallas_call(
        functools.partial(final_kernel, other),
        out_shape=pltpu.HBM(queries.shape, jnp.bfloat16),
        in_specs=[ANYWHERE, ANYWHERE, WHOLE, WHOLE, ANYWHERE if other else WHOLE],
        out_specs=ANYWHERE,
        scratch_shapes=[pltpu.VMEM((half, rows, width), jnp.bfloat16)] * 3
        + [pltpu.SemaphoreType.DMA((half,))] * 3,
        input_output_aliases={4: 0} if other else {},
        compiler_params=pltpu.CompilerParams(vmem_limit_bytes=16 * MIB),
        cost_estimate=pl.CostEstimate(
            flops=2 * half * rows * width * width,
            bytes_accessed=half * rows * width * 6,
            transcendentals=0,
        ),
        name="finish",
    )(
        in_hbm(queries),
        in_hbm(partial),
        in_vmem(weights),
        in_vmem(carried),
        in_hbm(extra) if other else in_vmem(extra),
    )


def shards(queries, keys, values, starts, lengths):
    width = queries.shape[2]
    scale = 1.0 / math.sqrt(width)
    chips = lax.axis_size("outer") * lax.axis_size("z")
    swap = [(0, 1), (1, 0)]

    theirs = block_states(starts, keys, values, True)
    got = lax.ppermute(theirs, "core", swap)
    own = block_states(starts, keys, values, False)
    parts = chip_states(own, got, chips)
    parts = lax.all_to_all(parts.reshape(chips, 1, -1), ("outer", "z"), 0, 0, tiled=True)
    parts = parts.reshape(-1, width)
    mine, weights, done = inside(starts, lengths, queries, keys, values, scale, False)
    befores = scan_chips(parts, done, chips)
    before = lax.all_to_all(befores, ("outer", "z"), 0, 0, tiled=True)
    rest, _, done = inside(starts, lengths, queries, keys, values, scale, True)
    before = before.reshape(-1, width)
    send = carried_to_send(before, own, done)
    carried = lax.ppermute(send, "core", swap)
    out = finish(queries, mine, weights, before, False, got)
    return finish(queries, rest, weights, carried, True, out)


def solution(mesh):
    outer, inner = mesh.shape["outer"], mesh.shape["inner"]
    chips = Mesh(np.asarray(mesh.devices).reshape(outer, inner // 2, 2), ("outer", "z", "core"))
    everywhere = ("outer", "z", "core")
    return jax.shard_map(
        shards,
        mesh=chips,
        in_specs=(P(None, everywhere, None),) * 3 + (P(everywhere),) * 2,
        out_specs=P(None, everywhere, None),
        check_vma=False,
    )
```

```python
import functools
import math

import jax
import jax.numpy as jnp
import numpy as np
from jax import lax
from jax.experimental import pallas as pl
from jax.experimental.pallas import tpu as pltpu
from jax.sharding import Mesh
from jax.sharding import PartitionSpec as P

CHUNK = 256
MIB = 1 << 20
PIECES = 4
MARKS = 16


def rows_of(first, shape):
    return first + lax.broadcasted_iota(jnp.int32, shape, 0)


def in_hbm(x):
    return pltpu.with_memory_space_constraint(x, pltpu.HBM)


def in_vmem(x):
    return pltpu.with_memory_space_constraint(x, pltpu.VMEM)


def half_of(other):
    core = lax.axis_index("core")
    return 1 - core if other else core


def grouped(count, size):
    return [range(h, min(h + size, count)) for h in range(0, count, size)]


SCALAR = pl.BlockSpec(memory_space=pltpu.SMEM)
WHOLE = pl.BlockSpec(memory_space=pltpu.VMEM)
ANYWHERE = pl.BlockSpec(memory_space=pl.ANY)


def state_kernel(other, start_ref, k_hbm, v_hbm, s_ref, k_ref, v_ref, mask_ref, k_sems, v_sems):
    half, length, width = k_ref.shape
    base = half_of(other) * half
    copies = []
    for h in range(half):
        pair = (
            pltpu.make_async_copy(k_hbm.at[base + h], k_ref.at[h], k_sems.at[h]),
            pltpu.make_async_copy(v_hbm.at[base + h], v_ref.at[h], v_sems.at[h]),
        )
        for copy in pair:
            copy.start()
        copies.append(pair)
    start = start_ref[0]
    begin = jnp.where(start < length, start, 0)
    kept = rows_of(0, (length, width)) >= begin
    mask_ref[...] = jnp.where(kept, 1.0, 0.0).astype(mask_ref.dtype)
    reset = jnp.where(start < length, 1.0, 0.0)
    first = jnp.where(lax.axis_index("core") == 0, 1.0, 0.0)
    s_ref[-16:-8, :] = jnp.full((8, width), reset, jnp.float32)
    s_ref[-8:, :] = jnp.full((8, width), first, jnp.float32)
    for group in grouped(half, 3):
        for h in group:
            for copy in copies[h]:
                copy.wait()
        for h in group:
            s_ref[h * width : (h + 1) * width, :] = jnp.dot(
                k_ref[h].T, v_ref[h] * mask_ref[...], preferred_element_type=jnp.float32
            )


def block_states(starts, keys, values, other):
    count, length, width = keys.shape
    half = count // 2
    rows = half * width + MARKS
    return pl.pallas_call(
        functools.partial(state_kernel, other),
        out_shape=pltpu.VMEM((rows, width), jnp.float32),
        in_specs=[SCALAR, ANYWHERE, ANYWHERE],
        out_specs=WHOLE,
        scratch_shapes=[
            pltpu.VMEM((half, length, width), jnp.bfloat16),
            pltpu.VMEM((half, length, width), jnp.bfloat16),
            pltpu.VMEM((length, width), jnp.bfloat16),
            pltpu.SemaphoreType.DMA((half,)),
            pltpu.SemaphoreType.DMA((half,)),
        ],
        compiler_params=pltpu.CompilerParams(vmem_limit_bytes=16 * MIB),
        cost_estimate=pl.CostEstimate(
            flops=count * length * width * width,
            bytes_accessed=count * length * width * 2,
            transcendentals=0,
        ),
        name="states",
    )(starts, in_hbm(keys), in_hbm(values))


def marks(ref):
    return ref[-16:-8, :], ref[-8:, :]


def tiles(x):
    return x.reshape(x.shape[0] // 8, 8, x.shape[1])


def chip_kernel(slices, own_ref, got_ref, out_hbm, out_ref, sems):
    own_reset, first = marks(own_ref)
    got_reset, _ = marks(got_ref)
    own_part = 1.0 - first * got_reset
    got_part = 1.0 - (1.0 - first) * own_reset
    mark = jnp.maximum(got_reset, own_reset)
    data = (own_ref.shape[0] - MARKS) // slices
    rows = data + 1
    group = slices // PIECES
    copies = []
    for n in range(PIECES):
        here = slice(n * group * data, (n + 1) * group * data)
        total = tiles(own_ref[here, :]) * own_part[None] + tiles(got_ref[here, :]) * got_part[None]
        total = total.reshape(group * data, -1)
        for p in range(group):
            first_row = (n * group + p) * rows
            out_ref[first_row : first_row + data, :] = total[p * data : (p + 1) * data, :]
            out_ref[first_row + data : first_row + rows, :] = mark[:1, :]
        there = slice(n * group * rows, (n + 1) * group * rows)
        copy = pltpu.make_async_copy(out_ref.at[there], out_hbm.at[there], sems.at[n])
        copy.start()
        copies.append(copy)
    for copy in copies:
        copy.wait()


def chip_states(own, got, slices):
    rows, width = own.shape
    shape = (rows - MARKS + slices, width)
    return pl.pallas_call(
        functools.partial(chip_kernel, slices),
        out_shape=pltpu.HBM(shape, jnp.float32),
        in_specs=[WHOLE, WHOLE],
        out_specs=ANYWHERE,
        scratch_shapes=[pltpu.VMEM(shape, jnp.float32), pltpu.SemaphoreType.DMA((PIECES,))],
        compiler_params=pltpu.CompilerParams(vmem_limit_bytes=8 * MIB),
        name="chip_states",
    )(in_vmem(own), in_vmem(got))


def scan_kernel(part_ref, after_ref, out_hbm, out_ref, sems):
    slices, data, width = out_ref.shape
    group = slices // PIECES
    before = jnp.zeros((data, width), jnp.float32)
    copies = []
    for n in range(PIECES):
        there = slice(n * group, (n + 1) * group)
        for c in range(slices)[there]:
            out_ref[c] = before
            first = c * (data + 1)
            reset = part_ref[first + data : first + data + 1, :]
            before = before * (1.0 - reset) + part_ref[first : first + data, :]
        copy = pltpu.make_async_copy(out_ref.at[there], out_hbm.at[there], sems.at[n])
        copy.start()
        copies.append(copy)
    for copy in copies:
        copy.wait()


def scan_chips(parts, after, slices):
    rows, width = parts.shape
    shape = (slices, rows // slices - 1, width)
    return pl.pallas_call(
        scan_kernel,
        out_shape=pltpu.HBM(shape, jnp.float32),
        in_specs=[WHOLE, ANYWHERE],
        out_specs=ANYWHERE,
        scratch_shapes=[pltpu.VMEM(shape, jnp.float32), pltpu.SemaphoreType.DMA((PIECES,))],
        compiler_params=pltpu.CompilerParams(vmem_limit_bytes=8 * MIB),
        name="scan_chips",
    )(in_vmem(parts), after)


def send_kernel(before_ref, own_ref, after_ref, out_ref):
    reset, first = marks(own_ref)
    data, width = out_ref.shape
    kept, added = 1.0 - first * reset, first
    total = tiles(before_ref[...]) * kept[None] + tiles(own_ref[:data, :]) * added[None]
    out_ref[...] = total.reshape(data, width)


def carried_to_send(before, own, after):
    return pl.pallas_call(
        send_kernel,
        out_shape=pltpu.VMEM(before.shape, jnp.float32),
        in_specs=[WHOLE, WHOLE, ANYWHERE],
        out_specs=WHOLE,
        compiler_params=pltpu.CompilerParams(vmem_limit_bytes=8 * MIB),
        name="carried_to_send",
    )(in_vmem(before), in_vmem(own), after)


def inside_kernel(
    heads,
    scale,
    start_ref,
    length_ref,
    q_ref,
    k_ref,
    v_ref,
    o_ref,
    weight_ref,
    token_ref,
    pair_ref,
    query_ref,
    key_ref,
    root_ref,
):
    rows, width = q_ref.shape[1], q_ref.shape[2]
    chunks = rows // CHUNK

    @pl.when(pl.program_id(0) == 0)
    def _():
        start, length = start_ref[0], length_ref[0]
        offsets = rows_of(0, (rows, width))
        counts = jnp.where(offsets < start, length + offsets + 1, offsets - start + 1)
        root = 1.0 / jnp.sqrt(counts.astype(jnp.float32))
        root_ref[...] = root
        weight_ref[...] = jnp.where(offsets < start, root * scale, 0.0)
        token_ref[...] = jnp.zeros_like(token_ref)
        for i in range(chunks):
            low = i * CHUNK
            inner = (start >= low) & (start < low + CHUNK)
            t = rows_of(low, (CHUNK, CHUNK))
            s = low + lax.broadcasted_iota(jnp.int32, (CHUNK, CHUNK), 1)
            allowed = (s <= t) & ((t < start) == (s < start))
            pair_ref[i] = jnp.where(allowed, scale, 0.0)
            t = rows_of(low, (CHUNK, width))
            cut = jnp.where(inner, start, low + CHUNK)
            query_ref[i] = jnp.where(t < cut, 1.0, 0.0).astype(query_ref.dtype)
            begin = jnp.where(inner, start, low)
            key_ref[i] = jnp.where(t >= begin, 1.0, 0.0).astype(key_ref.dtype)

    start = start_ref[0]
    states = [None] * heads
    for i in range(chunks):
        low = i * CHUNK
        here = slice(low, low + CHUNK)
        inner = (start >= low) & (start < low + CHUNK)
        scores = []
        for h in range(heads):
            product = lax.dot_general(
                q_ref[h, here, :],
                k_ref[h, here, :],
                (((1,), (1,)), ((), ())),
                preferred_element_type=jnp.float32,
            )
            scores.append((product * pair_ref[i]).astype(jnp.bfloat16))
        for h in range(heads):
            q, k, v = q_ref[h, here, :], k_ref[h, here, :], v_ref[h, here, :]
            total = jnp.dot(scores[h], v, preferred_element_type=jnp.float32)
            if i > 0:
                past = (states[h] * scale).astype(jnp.bfloat16)
                masked = q * query_ref[i]
                total += jnp.dot(masked, past, preferred_element_type=jnp.float32)
            o_ref[h, here, :] = (total * root_ref[here, :]).astype(o_ref.dtype)
            if i < chunks - 1:
                new = jnp.dot(k.T, v * key_ref[i], preferred_element_type=jnp.float32)
                states[h] = new if i == 0 else new + states[h] * jnp.where(inner, 0.0, 1.0)


def inside(starts, lengths, queries, keys, values, scale, other, heads=4):
    count, rows, width = queries.shape
    chunks = rows // CHUNK
    half = count // 2
    steps = half // heads
    given = pl.BlockSpec((heads, rows, width), lambda i: (half_of(other) * steps + i, 0, 0))
    return pl.pallas_call(
        functools.partial(inside_kernel, heads, scale),
        out_shape=(
            pltpu.HBM((half, rows, width), jnp.bfloat16),
            jax.ShapeDtypeStruct((rows, width), jnp.float32),
            jax.ShapeDtypeStruct((8, width), jnp.float32),
        ),
        grid=(steps,),
        in_specs=[SCALAR, SCALAR, given, given, given],
        out_specs=(
            pl.BlockSpec((heads, rows, width), lambda i: (i, 0, 0)),
            pl.BlockSpec((rows, width), lambda i: (0, 0)),
            pl.BlockSpec((8, width), lambda i: (0, 0)),
        ),
        scratch_shapes=[
            pltpu.VMEM((chunks, CHUNK, CHUNK), jnp.float32),
            pltpu.VMEM((chunks, CHUNK, width), jnp.bfloat16),
            pltpu.VMEM((chunks, CHUNK, width), jnp.bfloat16),
            pltpu.VMEM((rows, width), jnp.float32),
        ],
        compiler_params=pltpu.CompilerParams(vmem_limit_bytes=24 * MIB),
        cost_estimate=pl.CostEstimate(
            flops=half * rows * width * (4 * CHUNK + 4 * width),
            bytes_accessed=half * rows * width * 8,
            transcendentals=0,
        ),
        name="inside",
    )(starts, lengths, in_hbm(queries), in_hbm(keys), in_hbm(values))


def final_kernel(other, *refs):
    if other:
        q_ref, o_ref, w_ref, carried_ref, _, out_hbm, made_ref, out_sems = refs
    else:
        q_hbm, o_hbm, rest_hbm, w_ref, carried_ref, got_ref, out_hbm, next_q_ref, next_o_ref = refs[:9]
        q_ref, o_ref, made_ref, out_sems, q_sems, o_sems, next_q_sems, next_o_sems = refs[9:]
        reset, mate = marks(got_ref)
        kept, added = 1.0 - mate * reset, mate
    half, rows, width = made_ref.shape
    base = half_of(other) * half
    loads, pending = [], []
    if not other:
        next_base = half_of(True) * half
        for h in range(half):
            pair = (
                pltpu.make_async_copy(q_hbm.at[base + h], q_ref.at[h], q_sems.at[h]),
                pltpu.make_async_copy(o_hbm.at[h], o_ref.at[h], o_sems.at[h]),
            )
            for copy in pair:
                copy.start()
            loads.append(pair)
    nothing = jnp.zeros((width, width), jnp.bfloat16)

    def carried(h):
        here = slice(h * width, (h + 1) * width)
        total = carried_ref[here, :]
        if not other:
            total = tiles(total) * kept[None] + tiles(got_ref[here, :]) * added[None]
        return total.reshape(width, width).astype(jnp.bfloat16)

    fours = [range(h, h + 4) for h in range(2, half - 2, 4)]
    for group in [range(2), *fours, range(half - 2, half)]:
        if not other:
            for h in group:
                for copy in loads[h]:
                    copy.wait()
            for h in group:
                for copy in (
                    pltpu.make_async_copy(
                        q_hbm.at[next_base + h], next_q_ref.at[h], next_q_sems.at[h]
                    ),
                    pltpu.make_async_copy(rest_hbm.at[h], next_o_ref.at[h], next_o_sems.at[h]),
                ):
                    copy.start()
                    pending.append(copy)
        for h in group[::2]:
            both = jnp.concatenate(
                [
                    jnp.concatenate([carried(h), nothing], axis=1),
                    jnp.concatenate([nothing, carried(h + 1)], axis=1),
                ],
                axis=0,
            )
            pair = jnp.concatenate([q_ref[h], q_ref[h + 1]], axis=1)
            across = jnp.dot(pair, both, preferred_element_type=jnp.float32)
            for k in range(2):
                part = across[:, k * width : (k + 1) * width]
                total = o_ref[h + k].astype(jnp.float32) + part * w_ref[...]
                made_ref[h + k] = total.astype(made_ref.dtype)
        for h in group:
            store = pltpu.make_async_copy(made_ref.at[h], out_hbm.at[base + h], out_sems.at[h])
            store.start()
            pending.append(store)
    for copy in pending:
        copy.wait()


def finish_own(queries, partial, rest, weights, before, got):
    count, rows, width = queries.shape
    half = count // 2
    fetched = pltpu.VMEM((half, rows, width), jnp.bfloat16)
    return pl.pallas_call(
        functools.partial(final_kernel, False),
        out_shape=(pltpu.HBM(queries.shape, jnp.bfloat16), fetched, fetched),
        in_specs=[ANYWHERE] * 3 + [WHOLE] * 3,
        out_specs=(ANYWHERE, WHOLE, WHOLE),
        scratch_shapes=[pltpu.VMEM((half, rows, width), jnp.bfloat16)] * 3
        + [pltpu.SemaphoreType.DMA((half,))] * 5,
        compiler_params=pltpu.CompilerParams(vmem_limit_bytes=16 * MIB),
        cost_estimate=pl.CostEstimate(
            flops=2 * half * rows * width * width,
            bytes_accessed=half * rows * width * 10,
            transcendentals=0,
        ),
        name="finish_own",
    )(
        in_hbm(queries),
        in_hbm(partial),
        in_hbm(rest),
        in_vmem(weights),
        in_vmem(before),
        in_vmem(got),
    )


def finish_rest(queries, partial, weights, carried, out):
    half, rows, width = queries.shape
    return pl.pallas_call(
        functools.partial(final_kernel, True),
        out_shape=pltpu.HBM(out.shape, jnp.bfloat16),
        in_specs=[WHOLE] * 4 + [ANYWHERE],
        out_specs=ANYWHERE,
        scratch_shapes=[
            pltpu.VMEM((half, rows, width), jnp.bfloat16),
            pltpu.SemaphoreType.DMA((half,)),
        ],
        input_output_aliases={4: 0},
        compiler_params=pltpu.CompilerParams(vmem_limit_bytes=16 * MIB),
        cost_estimate=pl.CostEstimate(
            flops=2 * half * rows * width * width,
            bytes_accessed=half * rows * width * 2,
            transcendentals=0,
        ),
        name="finish_rest",
    )(in_vmem(queries), in_vmem(partial), in_vmem(weights), in_vmem(carried), in_hbm(out))


def shards(queries, keys, values, starts, lengths):
    width = queries.shape[2]
    scale = 1.0 / math.sqrt(width)
    chips = lax.axis_size("outer") * lax.axis_size("z")
    swap = [(0, 1), (1, 0)]

    theirs = block_states(starts, keys, values, True)
    got = lax.ppermute(theirs, "core", swap)
    own = block_states(starts, keys, values, False)
    parts = chip_states(own, got, chips)
    parts = lax.all_to_all(parts.reshape(chips, 1, -1), ("outer", "z"), 0, 0, tiled=True)
    parts = parts.reshape(-1, width)
    mine, weights, done = inside(starts, lengths, queries, keys, values, scale, False)
    befores = scan_chips(parts, done, chips)
    before = lax.all_to_all(befores, ("outer", "z"), 0, 0, tiled=True)
    rest, _, done = inside(starts, lengths, queries, keys, values, scale, True)
    before = before.reshape(-1, width)
    send = carried_to_send(before, own, done)
    carried = lax.ppermute(send, "core", swap)
    out, rest_q, rest_o = finish_own(queries, mine, rest, weights, before, got)
    return finish_rest(rest_q, rest_o, weights, carried, out)


def solution(mesh):
    outer, inner = mesh.shape["outer"], mesh.shape["inner"]
    chips = Mesh(np.asarray(mesh.devices).reshape(outer, inner // 2, 2), ("outer", "z", "core"))
    everywhere = ("outer", "z", "core")
    return jax.shard_map(
        shards,
        mesh=chips,
        in_specs=(P(None, everywhere, None),) * 3 + (P(everywhere),) * 2,
        out_specs=P(None, everywhere, None),
        check_vma=False,
    )
```
